512 devices in a mesh: blk: 128 (over z, y, core), grp: 4 (over x).
Axes of the slice: x: 4, y: 4, z: 16, core: 2. Of those that a mesh axis runs over, the one named last changes fastest.
Arguments:
- voxels: bfloat16 [1024, 64, 64, 128], P('blk', 'grp'), may hold values from -6 to 6
- shell_lo: int32 [1024, 64], P('blk', 'grp'), may hold values from 0 to 127, as said below
- shell_hi: int32 [1024, 64], P('blk', 'grp'), may hold values from 1 to 128, as said below
- conv_weight: bfloat16 [3, 3, 3, 64, 64], replicated, may hold values from -0.15625 to 0.15625
- conv_bias: float32 [64], replicated, may hold values from -3 to 3
- down_weight: bfloat16 [8, 64, 128], replicated, may hold values from -0.25 to 0.25
- down_bias: float32 [128], replicated, may hold values from -3 to 3
- coarse_owner: int32 [64, 4, 8], P(None, 'grp'), may hold values from 0 to 127, as said below
Outputs:
- coarse_out: bfloat16 [128, 4, 4, 128, 512], P('blk', 'grp')
The draws below stay inside these ranges and needn't reach their ends.
Inputs may be any that keep to these rules, and one draw needn't show every extreme that they name: shell_lo is below shell_hi in every voxel column. shell_hi is above shell_lo in every voxel column. `coarse_owner`: for each coarse column X and each index g of grp, the 8 coarse blocks have the owners (2 * X + k) mod the size of blk, for every whole k from -(3) up to 4, each k once.
All inputs are finite; a program needn't handle non-finite values.
Results may differ from the reference program's by a relative error of at most 0.0043.
Values may be sent and summed in bfloat16 or wider, within the bound.
No kernel may reach another device: no remote copies, remote signals or barrier semaphores. Data moves between devices by JAX's collectives and lax.ppermute only.
A program may use at most 64 MiB of HBM per device.

```python
import jax
import jax.numpy as jnp
from jax import lax

C = 64
CO = 128
BS = 8
YB = 2
ZV = 128
XN = 1024
YN = 64
XC = 64
NCZ = 8
HALF = 4
N_BLK = 128
N_GRP = 4


def shell_pair(key):
    key = jax.random.fold_in(key, 7)
    key_base, key_thick, key_low, key_high = jax.random.split(key, 4)
    blocks_x = XN // BS
    blocks_y = YN // BS
    base = jax.random.randint(key_base, (blocks_x, blocks_y), 0, ZV // 2)
    thick = jax.random.randint(key_thick, (blocks_x, blocks_y), ZV // 16, ZV // 2 + 1)
    base_full = jnp.repeat(jnp.repeat(base, BS, axis=0), BS, axis=1)
    thick_full = jnp.repeat(jnp.repeat(thick, BS, axis=0), BS, axis=1)
    jitter_low = jax.random.randint(key_low, (XN, YN), 0, ZV // 16 + 1)
    jitter_high = jax.random.randint(key_high, (XN, YN), 0, ZV // 16 + 1)
    lowest = base_full + jitter_low
    highest = jnp.minimum(lowest + thick_full + jitter_high, ZV)
    index_x = lax.broadcasted_iota(jnp.int32, (XN, YN), 0)
    index_y = lax.broadcasted_iota(jnp.int32, (XN, YN), 1)
    corner = (index_x == 0) & (index_y == 0)
    lowest = jnp.where(corner, 0, lowest)
    highest = jnp.where(corner, ZV, highest)
    top_cell = (index_x == XN - 1) & (index_y == YN - 1)
    lowest = jnp.where(top_cell, ZV - 1, lowest)
    highest = jnp.where(top_cell, ZV, highest)
    bottom_cell = (index_x == XN - 1) & (index_y == 0)
    lowest = jnp.where(bottom_cell, 0, lowest)
    highest = jnp.where(bottom_cell, 1, highest)
    return (lowest.astype(jnp.int32), highest.astype(jnp.int32))


def draw_shell_lo(key, part):
    return shell_pair(key)[0]


def draw_shell_hi(key, part):
    return shell_pair(key)[1]


def draw_coarse_owner(key, part):
    key = jax.random.fold_in(key, 11)
    groups = YN // (YB * BS)
    shape = (XC, groups, NCZ)
    scores = jax.random.randint(key, shape, 0, 1 << 20) * NCZ + lax.broadcasted_iota(jnp.int32, shape, 2)
    ordering = jnp.argsort(scores, axis=-1, stable=True).astype(jnp.int32)
    offsets = ordering - (NCZ // 2 - 1)
    column = lax.broadcasted_iota(jnp.int32, shape, 0)
    return ((2 * column + offsets) % (2 * XC)).astype(jnp.int32)


def shard_levels(stream_key, dims, cuts, least, high):
    def one(axis_at, parts):
        draws = jax.random.uniform(jax.random.fold_in(jax.random.fold_in(stream_key, 6), axis_at), (parts,), jnp.float32, least / len(cuts), high / len(cuts))
        return jnp.repeat(jnp.exp(draws), dims[axis_at] // parts).reshape((-1,) + (1,) * (len(dims) - axis_at - 1))

    factor_of = one(*cuts[0])
    for cut in cuts[1:]:
        factor_of = factor_of * one(*cut)
    return factor_of


def centred(stream_key, shape, spread, most, shards=(), kind=jnp.bfloat16):
    drawn = spread * jax.random.normal(stream_key, shape, jnp.float32)
    if shards:
        drawn = drawn * shard_levels(stream_key, shape, shards, -0.22, 0.18)
    return jnp.clip(drawn, -most, most).astype(kind)


def setup_inputs(seed: int = 0) -> dict:
    streams_of = jax.random.split(jax.random.key(seed), 9)
    return {
        "voxels": centred(streams_of[0], (XN, YN, C, ZV), 1.0, 6.0, ((0, 128), (1, 4))),
        "shell_lo": draw_shell_lo(jax.random.fold_in(streams_of[8], 71), 0),
        "shell_hi": draw_shell_hi(jax.random.fold_in(streams_of[8], 71), 0),
        "conv_weight": centred(streams_of[3], (3, 3, 3, C, C), (27 * C) ** -0.5, 0.15625),
        "conv_bias": centred(streams_of[4], (C,), 0.5, 3.0, (), jnp.float32),
        "down_weight": centred(streams_of[5], (8, C, CO), (8 * C) ** -0.5, 0.25),
        "down_bias": centred(streams_of[6], (CO,), 0.5, 3.0, (), jnp.float32),
        "coarse_owner": draw_coarse_owner(jax.random.fold_in(streams_of[8], 71), 0),
    }


def reference(voxels, shell_lo, shell_hi, conv_weight, conv_bias, down_weight, down_bias, coarse_owner):
    heights = lax.broadcasted_iota(jnp.int32, (XN, YN, ZV), 2)
    inside = (heights >= shell_lo[:, :, None]) & (heights < shell_hi[:, :, None])
    occupied = inside.astype(jnp.float32)
    masked = voxels.astype(jnp.float32) * occupied[:, :, None, :]
    padded = jnp.pad(masked, ((1, 1), (1, 1), (0, 0), (1, 1)))
    kernel = conv_weight.astype(jnp.float32)
    weights = down_weight.astype(jnp.float32).reshape(2, 2, 2, C, CO)
    fine_span = 2 * BS

    def one_column(column):
        slab_x = lax.dynamic_slice_in_dim(padded, column * fine_span, fine_span + 2, 0)
        summed = lax.conv_general_dilated(slab_x[None], kernel, (1, 1, 1), "VALID", dimension_numbers=("NXYCZ", "XYZIO", "NXYCZ"), precision=lax.Precision.HIGHEST)[0]
        kept_mask = lax.dynamic_slice_in_dim(occupied, column * fine_span, fine_span, 0)
        hidden = (jax.nn.silu(summed + conv_bias[None, None, :, None]) * kept_mask[:, :, None, :]).astype(jnp.bfloat16)
        children = hidden.astype(jnp.float32).reshape(BS, 2, YN // 2, 2, C, ZV // 2, 2)
        coarse = jnp.einsum("aibjcdk,ijkco->abod", children, weights, precision=lax.Precision.HIGHEST)
        coarse_mask = jnp.max(kept_mask.reshape(BS, 2, YN // 2, 2, ZV // 2, 2), axis=(1, 3, 5))
        coarse = ((coarse + down_bias[None, None, :, None]) * coarse_mask[:, :, None, :]).astype(jnp.bfloat16)
        blocks = coarse.reshape(BS, N_GRP, BS, CO, NCZ, BS).transpose(1, 4, 3, 0, 2, 5)
        return blocks.reshape(N_GRP, NCZ, CO, BS * BS * BS)

    all_blocks = lax.map(one_column, jnp.arange(XC, dtype=jnp.int32))
    owner_pos = jnp.arange(N_BLK, dtype=jnp.int32)
    first_col = (owner_pos - HALF + 1) // 2
    columns = (first_col[:, None] + jnp.arange(HALF, dtype=jnp.int32)[None, :]) % XC
    owner_rows = coarse_owner[columns]
    matches = owner_rows == owner_pos[:, None, None, None]
    levels = jnp.sum(jnp.where(matches, jnp.arange(NCZ, dtype=jnp.int32), 0), axis=-1).astype(jnp.int32)
    groups = jnp.arange(N_GRP, dtype=jnp.int32)
    result = all_blocks[columns[:, :, None], groups[None, None, :], levels]
    return result.transpose(0, 2, 1, 3, 4)
```

```python
import jax
import jax.numpy as jnp
from jax import lax
from jax.experimental import pallas as pl
from jax.experimental.pallas import tpu as pltpu
from jax.sharding import PartitionSpec as P

BF = jnp.bfloat16
F32 = jnp.float32
VMEM = pltpu.VMEM
SMEM = pltpu.SMEM


def prep_kernel(cw, cb, dw, db, w_out, d_out, cb_out, db_out, sel_out):
    zero = jnp.zeros((64, 64), F32)
    for dx in range(3):
        for dz in range(3):
            taps = [cw[dx, dy, dz].astype(F32) for dy in range(3)]
            for yo in range(2):
                line = ([zero] if yo else []) + taps + ([] if yo else [zero])
                for half in range(2):
                    pair = jnp.concatenate(line[2 * half : 2 * half + 2], axis=0)
                    row = (dz * 2 + yo) * 64
                    col = (dx * 4 + half * 2) * 64
                    w_out[row : row + 64, col : col + 128] = pair.T.astype(BF)
    for k in range(2):
        for i in range(2):
            pair = jnp.concatenate([dw[4 * i + k], dw[4 * i + 2 + k]], axis=0).astype(F32)
            d_out[k * 128 : k * 128 + 128, i * 128 : i * 128 + 128] = pair.T.astype(BF)
    cb_out[...] = jnp.broadcast_to(cb[...], (128, 128)).T
    db_out[...] = jnp.broadcast_to(db[...], (128, 128)).T
    for q in range(8):
        z = lax.broadcasted_iota(jnp.int32, (128, 512), 0)
        lane = lax.broadcasted_iota(jnp.int32, (128, 512), 1)
        want = jnp.where(((lane >> 3) & 7) == q, 16 * (lane >> 6) + 2 * (lane & 7), -1)
        sel_out[q * 128 : q * 128 + 128, :] = jnp.where(z == want, 1.0, 0.0).astype(BF)


def prep(conv_weight, conv_bias, down_weight, down_bias):
    return pl.pallas_call(
        prep_kernel,
        out_shape=(
            jax.ShapeDtypeStruct((384, 768), BF),
            jax.ShapeDtypeStruct((256, 256), BF),
            jax.ShapeDtypeStruct((128, 128), F32),
            jax.ShapeDtypeStruct((128, 128), F32),
            jax.ShapeDtypeStruct((1024, 512), BF),
        ),
        name="prep",
    )(
        conv_weight,
        jnp.tile(conv_bias, 2)[None],
        down_weight,
        down_bias[None],
    )


def main_kernel(
    lo, hi, slots, vox, ylo, yhi, xlo, xhi, w, d, cb, db, sel, keep, give, pad, cells, pieces
):
    lane8 = lax.broadcasted_iota(jnp.int32, (8, 128), 1)

    def occupied(x, y):
        return jnp.where((lane8 >= lo[x, y]) & (lane8 < hi[x, y]), 1.0, 0.0)

    pad[0] = xlo[...]
    pad[9] = xhi[...]
    for x in range(8):
        pad[x + 1, 0] = ylo[x]
        pad[x + 1, 17] = yhi[x]

    @pl.loop(0, 8)
    def _(x):
        for y in range(16):
            mask = jnp.concatenate([occupied(x, y)] * 2, axis=0).astype(BF)
            pad[x + 1, y + 1] = (vox[x, y].reshape(4, 16, 128) * mask[None]).reshape(64, 128)

    lane = lax.broadcasted_iota(jnp.int32, (128, 128), 1)

    def conv_cell(p, yp):
        rows = [pad[2 * p + r, pl.ds(2 * yp, 4)].reshape(256, 128) for r in range(4)]
        window = jnp.concatenate(
            [jnp.concatenate([rows[t], rows[t + 1]], axis=1) for t in range(3)], axis=0
        )
        summed = jnp.dot(w[...], window, preferred_element_type=F32)
        parts = []
        for xi in range(2):
            part = summed[:, xi * 128 : xi * 128 + 128]
            below = jnp.where(lane == 0, 0.0, pltpu.roll(part[0:128], 1, 1))
            above = jnp.where(lane == 127, 0.0, pltpu.roll(part[256:384], 127, 1))
            half = (below + above + part[128:256] + cb[...]) * 0.5
            act = half + half * jnp.tanh(half)
            masks = [occupied(2 * p + xi, 2 * yp + yo) for yo in range(2)]
            mask = jnp.stack(masks)[:, None]
            act = act.reshape(2, 8, 8, 128) * mask
            parts.append(act.reshape(128, 128).astype(BF))
        return jnp.concatenate(parts, axis=0)

    def coarse_mask(p, yp):
        found = None
        for xi in range(2):
            for yo in range(2):
                x, y = 2 * p + xi, 2 * yp + yo
                here = (lane8 + 1 >= lo[x, y]) & (lane8 < hi[x, y])
                found = here if found is None else found | here
        return jnp.where(found, 1.0, 0.0)

    @pl.loop(0, 4)
    def _(p):
        for ypp in range(4):
            hidden = jnp.concatenate([conv_cell(p, 2 * ypp), conv_cell(p, 2 * ypp + 1)], axis=1)
            down = jnp.dot(d[...], hidden, preferred_element_type=F32)
            for e in range(2):
                part = down[:, e * 128 : e * 128 + 128]
                total = part[0:128] + pltpu.roll(part[128:256], 127, 1) + db[...]
                total = total.reshape(16, 8, 128) * coarse_mask(p, 2 * ypp + e)[None]
                q = 2 * ypp + e
                cells[pl.ds(p * 128, 128), q * 128 : q * 128 + 128] = total.reshape(
                    128, 128
                ).astype(BF)

    for pair in range(2):
        picked = jnp.dot(
            cells[pair * 256 : pair * 256 + 256], sel[...], preferred_element_type=F32
        )
        for level in range(8):
            at = slice(level * 64, level * 64 + 64)
            both = jnp.concatenate([picked[0:128, at], picked[128:256, at]], axis=1)
            pieces[slots[level], :, pair * 128 : pair * 128 + 128] = both.astype(BF)
    keep[...] = pieces[0:4]
    give[...] = pieces[4:8]


def main(lo, hi, slots, vox, ylo, yhi, xlo, xhi, tables):
    half = jax.ShapeDtypeStruct((4, 128, 256), BF)
    smem = pl.BlockSpec(memory_space=SMEM)
    vmem = pl.BlockSpec(memory_space=VMEM)
    return pl.pallas_call(
        main_kernel,
        out_shape=(half, half),
        in_specs=[smem] * 3 + [vmem] * 10,
        out_specs=(vmem, vmem),
        scratch_shapes=[
            VMEM((10, 18, 64, 128), BF),
            VMEM((512, 1024), BF),
            VMEM((8, 128, 256), BF),
        ],
        compiler_params=pltpu.CompilerParams(vmem_limit_bytes=48 * 1024 * 1024),
        name="scene",
    )(lo, hi, slots, vox, ylo, yhi, xlo, xhi, *tables)


def ring(count, step):
    return [(i, step(i) % count) for i in range(count)]


def local(voxels, shell_lo, shell_hi, conv_weight, conv_bias, down_weight, down_bias, coarse_owner):
    blk_n = lax.axis_size("blk")
    grp_n = lax.axis_size("grp")
    me = lax.axis_index("blk")
    core = me % 2

    def masked(block, lo, hi):
        heights = lax.broadcasted_iota(jnp.int32, block.shape[:1] + block.shape[2:], 1)
        inside = (heights >= lo[:, None]) & (heights < hi[:, None])
        return block * inside.astype(BF)[:, None, :]

    up = [(i, i + 1) for i in range(grp_n - 1)]
    down = [(b, a) for a, b in up]
    ylo = lax.ppermute(masked(voxels[:, 15], shell_lo[:, 15], shell_hi[:, 15]), "grp", up)
    yhi = lax.ppermute(masked(voxels[:, 0], shell_lo[:, 0], shell_hi[:, 0]), "grp", down)
    tables = prep(conv_weight, conv_bias, down_weight, down_bias)

    def x_face(x):
        face = masked(voxels[x], shell_lo[x], shell_hi[x])
        return jnp.concatenate([ylo[x : x + 1], face, yhi[x : x + 1]], axis=0)

    ahead = [(i, i + 1) for i in range(blk_n - 1)]
    behind = [(b, a) for a, b in ahead]
    xlo = lax.ppermute(x_face(7), "blk", ahead)
    xhi = lax.ppermute(x_face(0), "blk", behind)

    column = me // 2
    owners = lax.dynamic_index_in_dim(coarse_owner[:, 0, :], column, 0, keepdims=False)
    offset = (owners - 2 * column + 3) % blk_n
    slots = (offset + 4 * core) % 8

    keep, give = main(shell_lo, shell_hi, slots, voxels, ylo, yhi, xlo, xhi, tables)
    got = lax.ppermute(give, "blk", ring(blk_n, lambda i: i ^ 1))
    even = core == 0
    whole = jnp.where(
        even, jnp.concatenate([keep, got], axis=2), jnp.concatenate([got, keep], axis=2)
    )
    def mine(a, b):
        return jnp.where(even, whole[a], whole[b])

    one = lax.ppermute(mine(2, 1), "blk", ring(blk_n, lambda i: i + 1 if i % 2 else i - 1))
    two = lax.ppermute(mine(1, 2), "blk", ring(blk_n, lambda i: i + 2 if i % 2 else i - 2))
    three = lax.ppermute(mine(0, 3), "blk", ring(blk_n, lambda i: i + 3 if i % 2 else i - 3))
    stay = mine(3, 0)
    result = jnp.stack(
        [
            jnp.where(even, three, two),
            jnp.where(even, one, stay),
            jnp.where(even, stay, one),
            jnp.where(even, two, three),
        ]
    )
    return result[None, None]


def solution(mesh):
    placed = (
        P("blk", "grp", None, None),
        P("blk", "grp"),
        P("blk", "grp"),
        P(),
        P(),
        P(),
        P(),
        P(None, "grp", None),
    )
    return jax.shard_map(
        local,
        mesh=mesh,
        in_specs=placed,
        out_specs=P("blk", "grp", None, None, None),
        check_vma=False,
    )
```

```python
import jax
import jax.numpy as jnp
from jax import lax
from jax.experimental import pallas as pl
from jax.experimental.pallas import tpu as pltpu
from jax.sharding import PartitionSpec as P

BF = jnp.bfloat16
F32 = jnp.float32
VMEM = pltpu.VMEM
SMEM = pltpu.SMEM


def small_vmem(mib):
    return pltpu.CompilerParams(vmem_limit_bytes=mib * 1024 * 1024)


def prep_kernel(cw, cb, dw, db, w_out, d_out, cb_out, db_out, sel_out):
    zero = jnp.zeros((64, 64), F32)
    for dx in range(3):
        for dz in range(3):
            taps = [cw[dx, dy, dz].astype(F32) for dy in range(3)]
            for yo in range(2):
                line = ([zero] if yo else []) + taps + ([] if yo else [zero])
                for half in range(2):
                    pair = jnp.concatenate(line[2 * half : 2 * half + 2], axis=0)
                    row = (dz * 2 + yo) * 64
                    col = (dx * 4 + half * 2) * 64
                    w_out[row : row + 64, col : col + 128] = pair.T.astype(BF)
    for k in range(2):
        for i in range(2):
            pair = jnp.concatenate([dw[4 * i + k], dw[4 * i + 2 + k]], axis=0).astype(F32)
            d_out[k * 128 : k * 128 + 128, i * 128 : i * 128 + 128] = pair.T.astype(BF)
    cb_out[...] = jnp.broadcast_to(cb[...], (128, 128)).T
    db_out[...] = jnp.broadcast_to(db[...], (128, 128)).T
    for q in range(8):
        z = lax.broadcasted_iota(jnp.int32, (128, 512), 0)
        lane = lax.broadcasted_iota(jnp.int32, (128, 512), 1)
        want = jnp.where(((lane >> 3) & 7) == q, 16 * (lane >> 6) + 2 * (lane & 7), -1)
        sel_out[q * 128 : q * 128 + 128, :] = jnp.where(z == want, 1.0, 0.0).astype(BF)


def prep(conv_weight, conv_bias, down_weight, down_bias):
    return pl.pallas_call(
        prep_kernel,
        out_shape=(
            jax.ShapeDtypeStruct((384, 768), BF),
            jax.ShapeDtypeStruct((256, 256), BF),
            jax.ShapeDtypeStruct((128, 128), F32),
            jax.ShapeDtypeStruct((128, 128), F32),
            jax.ShapeDtypeStruct((1024, 512), BF),
        ),
        compiler_params=small_vmem(8),
        cost_estimate=pl.CostEstimate(flops=10**9, bytes_accessed=4 * 10**6, transcendentals=0),
        name="prep",
    )(
        conv_weight,
        jnp.tile(conv_bias, 2)[None],
        down_weight,
        down_bias[None],
    )


def occupancy(lo, hi, x, y):
    lane = lax.broadcasted_iota(jnp.int32, (8, 128), 1)
    return jnp.where((lane >= lo[x, y]) & (lane < hi[x, y]), 1.0, 0.0)


def masked_column(column, lo, hi, x, y):
    mask = jnp.concatenate([occupancy(lo, hi, x, y)] * 2, axis=0).astype(BF)
    return (column.reshape(4, 16, 128) * mask[None]).reshape(64, 128)


def faces_kernel(lo, hi, vox, y_first, y_last, x_first, x_last, sems):
    copies = [
        pltpu.make_async_copy(vox.at[:, 0], y_first, sems.at[0]),
        pltpu.make_async_copy(vox.at[:, 15], y_last, sems.at[1]),
        pltpu.make_async_copy(vox.at[0], x_first, sems.at[2]),
        pltpu.make_async_copy(vox.at[7], x_last, sems.at[3]),
    ]
    for copy in copies:
        copy.start()
    for copy, ref, y in ((copies[0], y_first, 0), (copies[1], y_last, 15)):
        copy.wait()
        for x in range(8):
            ref[x] = masked_column(ref[x], lo, hi, x, y)
    for copy, ref, x in ((copies[2], x_first, 0), (copies[3], x_last, 7)):
        copy.wait()
        for y in range(16):
            ref[y] = masked_column(ref[y], lo, hi, x, y)


def faces(lo, hi, vox):
    y_face = jax.ShapeDtypeStruct((8, 64, 128), BF)
    x_face = jax.ShapeDtypeStruct((16, 64, 128), BF)
    smem = pl.BlockSpec(memory_space=SMEM)
    vmem = pl.BlockSpec(memory_space=VMEM)
    return pl.pallas_call(
        faces_kernel,
        out_shape=(y_face, y_face, x_face, x_face),
        in_specs=[smem, smem, pl.BlockSpec(memory_space=pltpu.HBM)],
        out_specs=(vmem,) * 4,
        scratch_shapes=[pltpu.SemaphoreType.DMA((4,))],
        compiler_params=small_vmem(4),
        name="faces",
    )(lo, hi, vox)


def scene_rows(starts, columns, lo, hi, pad, w, d, cb, db, sel, cells):
    lane8 = lax.broadcasted_iota(jnp.int32, (8, 128), 1)
    lane = lax.broadcasted_iota(jnp.int32, (128, 128), 1)

    def conv_cell(row, x, yp):
        rows = [pad[row + r, pl.ds(2 * yp, 4)].reshape(256, 128) for r in range(4)]
        window = jnp.concatenate(
            [jnp.concatenate([rows[t], rows[t + 1]], axis=1) for t in range(3)], axis=0
        )
        summed = jnp.dot(w[...], window, preferred_element_type=F32)
        parts = []
        for xi in range(2):
            part = summed[:, xi * 128 : xi * 128 + 128]
            below = jnp.where(lane == 0, 0.0, pltpu.roll(part[0:128], 1, 1))
            above = jnp.where(lane == 127, 0.0, pltpu.roll(part[256:384], 127, 1))
            half = (below + above + part[128:256] + cb[...]) * 0.5
            act = half + half * jnp.tanh(half)
            masks = [occupancy(lo, hi, x + xi, 2 * yp + yo) for yo in range(2)]
            act = act.reshape(2, 8, 8, 128) * jnp.stack(masks)[:, None]
            parts.append(act.reshape(128, 128).astype(BF))
        return jnp.concatenate(parts, axis=0)

    def coarse_mask(x0, yp):
        found = None
        for xi in range(2):
            for yo in range(2):
                x, y = x0 + xi, 2 * yp + yo
                here = (lane8 + 1 >= lo[x, y]) & (lane8 < hi[x, y])
                found = here if found is None else found | here
        return jnp.where(found, 1.0, 0.0)

    (row0, x0), (row1, x1) = starts

    @pl.loop(0, 2)
    def _(t):
        row = row0 + t * (row1 - row0)
        x = x0 + t * (x1 - x0)
        for ypp in range(4):
            hidden = jnp.concatenate(
                [conv_cell(row, x, 2 * ypp), conv_cell(row, x, 2 * ypp + 1)], axis=1
            )
            down = jnp.dot(d[...], hidden, preferred_element_type=F32)
            for e in range(2):
                q = 2 * ypp + e
                part = down[:, e * 128 : e * 128 + 128]
                total = part[0:128] + pltpu.roll(part[128:256], 127, 1) + db[...]
                total = total.reshape(16, 8, 128) * coarse_mask(x, q)[None]
                cells[pl.ds(t * 128, 128), q * 128 : q * 128 + 128] = total.reshape(
                    128, 128
                ).astype(BF)

    return jnp.dot(cells[...], sel[...], preferred_element_type=F32)


def inner_kernel(lo, hi, vox, ylo, yhi, w, d, cb, db, sel, out, pad, cells):
    for r in range(6):
        pad[r, 0] = ylo[r + 1]
        pad[r, 17] = yhi[r + 1]

    @pl.loop(0, 6)
    def _(r):
        for y in range(16):
            pad[r, y + 1] = masked_column(vox[r + 1, y], lo, hi, r + 1, y)

    out[...] = scene_rows(((0, 2), (2, 4)), None, lo, hi, pad, w, d, cb, db, sel, cells)


def outer_kernel(
    lo, hi, slots, vox, ylo, yhi, xlo, xhi, inner, w, d, cb, db, sel, keep, give, pad, cells, pieces
):
    pad[0] = xlo[...]
    pad[7] = xhi[...]
    for r in range(3):
        pad[r + 1, 0] = ylo[r]
        pad[r + 1, 17] = yhi[r]
        pad[r + 4, 0] = ylo[r + 5]
        pad[r + 4, 17] = yhi[r + 5]

    @pl.loop(0, 3)
    def _(r):
        for y in range(16):
            pad[r + 1, y + 1] = masked_column(vox[r, y], lo, hi, r, y)
            pad[r + 4, y + 1] = masked_column(vox[r + 5, y], lo, hi, r + 5, y)

    ends = scene_rows(((0, 0), (4, 6)), None, lo, hi, pad, w, d, cb, db, sel, cells)
    rows = (ends[0:128], inner[0:128], inner[128:256], ends[128:256])
    for pair in range(2):
        for level in range(8):
            at = slice(level * 64, level * 64 + 64)
            both = jnp.concatenate([rows[2 * pair][:, at], rows[2 * pair + 1][:, at]], axis=1)
            pieces[slots[level], :, pair * 128 : pair * 128 + 128] = both.astype(BF)
    keep[...] = pieces[0:4]
    give[...] = pieces[4:8]


def inner_rows(lo, hi, vox, ylo, yhi, tables):
    smem = pl.BlockSpec(memory_space=SMEM)
    vmem = pl.BlockSpec(memory_space=VMEM)
    return pl.pallas_call(
        inner_kernel,
        out_shape=jax.ShapeDtypeStruct((256, 512), F32),
        in_specs=[smem] * 2 + [vmem] * 8,
        out_specs=vmem,
        scratch_shapes=[VMEM((6, 18, 64, 128), BF), VMEM((256, 1024), BF)],
        compiler_params=small_vmem(12),
        cost_estimate=pl.CostEstimate(flops=5 * 10**9, bytes_accessed=4 * 10**6, transcendentals=0),
        name="inner",
    )(lo, hi, vox, ylo, yhi, *tables)


def outer_rows(lo, hi, slots, vox, ylo, yhi, xlo, xhi, inner, tables):
    half = jax.ShapeDtypeStruct((4, 128, 256), BF)
    smem = pl.BlockSpec(memory_space=SMEM)
    vmem = pl.BlockSpec(memory_space=VMEM)
    return pl.pallas_call(
        outer_kernel,
        out_shape=(half, half),
        in_specs=[smem] * 3 + [vmem] * 11,
        out_specs=(vmem, vmem),
        scratch_shapes=[
            VMEM((8, 18, 64, 128), BF),
            VMEM((256, 1024), BF),
            VMEM((8, 128, 256), BF),
        ],
        compiler_params=small_vmem(12),
        name="outer",
    )(lo, hi, slots, vox, ylo, yhi, xlo, xhi, inner, *tables)


def ring(count, step):
    return [(i, step(i) % count) for i in range(count)]


def local(voxels, shell_lo, shell_hi, conv_weight, conv_bias, down_weight, down_bias, coarse_owner):
    blk_n = lax.axis_size("blk")
    grp_n = lax.axis_size("grp")
    me = lax.axis_index("blk")
    core = me % 2

    up = [(i, i + 1) for i in range(grp_n - 1)]
    down = [(b, a) for a, b in up]
    y_first, y_last, x_first, x_last = faces(shell_lo, shell_hi, voxels)
    ylo = lax.ppermute(y_last, "grp", up)
    yhi = lax.ppermute(y_first, "grp", down)
    tables = prep(conv_weight, conv_bias, down_weight, down_bias)
    ylo, yhi, tables = lax.optimization_barrier((ylo, yhi, tables))

    ahead = [(i, i + 1) for i in range(blk_n - 1)]
    behind = [(b, a) for a, b in ahead]
    xlo = lax.ppermute(jnp.concatenate([ylo[7:8], x_last, yhi[7:8]]), "blk", ahead)
    xhi = lax.ppermute(jnp.concatenate([ylo[0:1], x_first, yhi[0:1]]), "blk", behind)
    inner = inner_rows(shell_lo, shell_hi, voxels, ylo, yhi, tables)

    column = me // 2
    owners = lax.dynamic_index_in_dim(coarse_owner[:, 0, :], column, 0, keepdims=False)
    offset = (owners - 2 * column + 3) % blk_n - 3
    place = jnp.where(offset <= 0, offset + 3, 4 - offset)
    slots = jnp.where((offset <= 0) == (core == 0), place, place + 4)

    keep, give = outer_rows(
        shell_lo, shell_hi, slots, voxels, ylo, yhi, xlo, xhi, inner, tables
    )
    got = lax.ppermute(give, "blk", ring(blk_n, lambda i: i ^ 1))
    even = core == 0
    whole = jnp.where(
        even, jnp.concatenate([keep, got], axis=2), jnp.concatenate([got, keep], axis=2)
    )
    near = lax.ppermute(whole[0:2], "blk", ring(blk_n, lambda i: i + 2 if i % 2 else i - 2))
    far = lax.ppermute(
        jnp.concatenate([near[0:1], whole[2:3]]),
        "blk",
        ring(blk_n, lambda i: i + 1 if i % 2 else i - 1),
    )
    result = jnp.where(
        even,
        jnp.stack([far[0], far[1], whole[3], near[1]]),
        jnp.stack([near[1], whole[3], far[1], far[0]]),
    )
    return result[None, None]


def solution(mesh):
    placed = (
        P("blk", "grp", None, None),
        P("blk", "grp"),
        P("blk", "grp"),
        P(),
        P(),
        P(),
        P(),
        P(None, "grp", None),
    )
    return jax.shard_map(
        local,
        mesh=mesh,
        in_specs=placed,
        out_specs=P("blk", "grp", None, None, None),
        check_vma=False,
    )
```

```python
import jax
import jax.numpy as jnp
from jax import lax
from jax.experimental import pallas as pl
from jax.experimental.pallas import tpu as pltpu
from jax.sharding import PartitionSpec as P

BF = jnp.bfloat16
F32 = jnp.float32
VMEM = pltpu.VMEM
SMEM = pltpu.SMEM


def small_vmem(mib):
    return pltpu.CompilerParams(vmem_limit_bytes=mib * 1024 * 1024)


def prep_kernel(cw, cb, dw, db, w_out, d_out, cb_out, db_out, sel_out):
    zero = jnp.zeros((64, 64), F32)
    for dx in range(3):
        for dz in range(3):
            taps = [cw[dx, dy, dz].astype(F32) for dy in range(3)]
            for yo in range(2):
                line = ([zero] if yo else []) + taps + ([] if yo else [zero])
                for half in range(2):
                    pair = jnp.concatenate(line[2 * half : 2 * half + 2], axis=0)
                    row = (dz * 2 + yo) * 64
                    col = (dx * 4 + half * 2) * 64
                    w_out[row : row + 64, col : col + 128] = pair.T.astype(BF)
    for k in range(2):
        for i in range(2):
            pair = jnp.concatenate([dw[4 * i + k], dw[4 * i + 2 + k]], axis=0).astype(F32)
            d_out[k * 128 : k * 128 + 128, i * 128 : i * 128 + 128] = pair.T.astype(BF)
    cb_out[...] = jnp.broadcast_to(cb[...], (128, 128)).T
    db_out[...] = jnp.broadcast_to(db[...], (128, 128)).T
    for q in range(8):
        z = lax.broadcasted_iota(jnp.int32, (128, 512), 0)
        lane = lax.broadcasted_iota(jnp.int32, (128, 512), 1)
        want = jnp.where(((lane >> 3) & 7) == q, 16 * (lane >> 6) + 2 * (lane & 7), -1)
        sel_out[q * 128 : q * 128 + 128, :] = jnp.where(z == want, 1.0, 0.0).astype(BF)


def prep(conv_weight, conv_bias, down_weight, down_bias):
    return pl.pallas_call(
        prep_kernel,
        out_shape=(
            jax.ShapeDtypeStruct((384, 768), BF),
            jax.ShapeDtypeStruct((256, 256), BF),
            jax.ShapeDtypeStruct((128, 128), F32),
            jax.ShapeDtypeStruct((128, 128), F32),
            jax.ShapeDtypeStruct((1024, 512), BF),
        ),
        compiler_params=small_vmem(8),
        cost_estimate=pl.CostEstimate(flops=10**9, bytes_accessed=4 * 10**6, transcendentals=0),
        name="prep",
    )(
        conv_weight,
        jnp.tile(conv_bias, 2)[None],
        down_weight,
        down_bias[None],
    )


def occupancy(lo, hi, x, y):
    lane = lax.broadcasted_iota(jnp.int32, (8, 128), 1)
    return jnp.where((lane >= lo[x, y]) & (lane < hi[x, y]), 1.0, 0.0)


def masked_column(column, lo, hi, x, y):
    mask = jnp.concatenate([occupancy(lo, hi, x, y)] * 2, axis=0).astype(BF)
    return (column.reshape(4, 16, 128) * mask[None]).reshape(64, 128)


def faces_kernel(lo, hi, vox, y_first, y_last, x_first, x_last, sems):
    copies = [
        pltpu.make_async_copy(vox.at[:, 0], y_first, sems.at[0]),
        pltpu.make_async_copy(vox.at[:, 15], y_last, sems.at[1]),
        pltpu.make_async_copy(vox.at[0], x_first, sems.at[2]),
        pltpu.make_async_copy(vox.at[7], x_last, sems.at[3]),
    ]
    for copy in copies:
        copy.start()
    for copy, ref, y in ((copies[0], y_first, 0), (copies[1], y_last, 15)):
        copy.wait()
        for x in range(8):
            ref[x] = masked_column(ref[x], lo, hi, x, y)
    for copy, ref, x in ((copies[2], x_first, 0), (copies[3], x_last, 7)):
        copy.wait()
        for y in range(16):
            ref[y] = masked_column(ref[y], lo, hi, x, y)


def faces(lo, hi, vox):
    y_face = jax.ShapeDtypeStruct((8, 64, 128), BF)
    x_face = jax.ShapeDtypeStruct((16, 64, 128), BF)
    smem = pl.BlockSpec(memory_space=SMEM)
    vmem = pl.BlockSpec(memory_space=VMEM)
    return pl.pallas_call(
        faces_kernel,
        out_shape=(y_face, y_face, x_face, x_face),
        in_specs=[smem, smem, pl.BlockSpec(memory_space=pltpu.HBM)],
        out_specs=(vmem,) * 4,
        scratch_shapes=[pltpu.SemaphoreType.DMA((4,))],
        compiler_params=small_vmem(4),
        name="faces",
    )(*(pltpu.with_memory_space_constraint(a, pltpu.HBM) for a in (lo, hi, vox)))


def scene_rows(starts, columns, lo, hi, pad, w, d, cb, db, sel, cells):
    lane8 = lax.broadcasted_iota(jnp.int32, (8, 128), 1)
    lane = lax.broadcasted_iota(jnp.int32, (128, 128), 1)

    def conv_cell(row, x, yp):
        rows = [pad[row + r, pl.ds(2 * yp, 4)].reshape(256, 128) for r in range(4)]
        window = jnp.concatenate(
            [jnp.concatenate([rows[t], rows[t + 1]], axis=1) for t in range(3)], axis=0
        )
        summed = jnp.dot(w[...], window, preferred_element_type=F32)
        parts = []
        for xi in range(2):
            part = summed[:, xi * 128 : xi * 128 + 128]
            below = jnp.where(lane == 0, 0.0, pltpu.roll(part[0:128], 1, 1))
            above = jnp.where(lane == 127, 0.0, pltpu.roll(part[256:384], 127, 1))
            half = (below + above + part[128:256] + cb[...]) * 0.5
            act = half + half * jnp.tanh(half)
            masks = [occupancy(lo, hi, x + xi, 2 * yp + yo) for yo in range(2)]
            act = act.reshape(2, 8, 8, 128) * jnp.stack(masks)[:, None]
            parts.append(act.reshape(128, 128).astype(BF))
        return jnp.concatenate(parts, axis=0)

    def coarse_mask(x0, yp):
        found = None
        for xi in range(2):
            for yo in range(2):
                x, y = x0 + xi, 2 * yp + yo
                here = (lane8 + 1 >= lo[x, y]) & (lane8 < hi[x, y])
                found = here if found is None else found | here
        return jnp.where(found, 1.0, 0.0)

    (row0, x0), (row1, x1) = starts

    @pl.loop(0, 2)
    def _(t):
        row = row0 + t * (row1 - row0)
        x = x0 + t * (x1 - x0)
        for ypp in range(4):
            hidden = jnp.concatenate(
                [conv_cell(row, x, 2 * ypp), conv_cell(row, x, 2 * ypp + 1)], axis=1
            )
            down = jnp.dot(d[...], hidden, preferred_element_type=F32)
            for e in range(2):
                q = 2 * ypp + e
                part = down[:, e * 128 : e * 128 + 128]
                total = part[0:128] + pltpu.roll(part[128:256], 127, 1) + db[...]
                total = total.reshape(16, 8, 128) * coarse_mask(x, q)[None]
                cells[pl.ds(t * 128, 128), q * 128 : q * 128 + 128] = total.reshape(
                    128, 128
                ).astype(BF)

    return jnp.dot(cells[...], sel[...], preferred_element_type=F32)


def inner_kernel(lo, hi, vox, ylo, yhi, w, d, cb, db, sel, out, pad, cells):
    for r in range(6):
        pad[r, 0] = ylo[r + 1]
        pad[r, 17] = yhi[r + 1]

    @pl.loop(0, 6)
    def _(r):
        for y in range(16):
            pad[r, y + 1] = masked_column(vox[r + 1, y], lo, hi, r + 1, y)

    out[...] = scene_rows(((0, 2), (2, 4)), None, lo, hi, pad, w, d, cb, db, sel, cells)


def outer_kernel(
    lo, hi, slots, vox, ylo, yhi, xlo, xhi, inner, w, d, cb, db, sel, keep, give, pad, cells, pieces
):
    pad[0] = xlo[...]
    pad[7] = xhi[...]
    for r in range(3):
        pad[r + 1, 0] = ylo[r]
        pad[r + 1, 17] = yhi[r]
        pad[r + 4, 0] = ylo[r + 5]
        pad[r + 4, 17] = yhi[r + 5]

    @pl.loop(0, 3)
    def _(r):
        for y in range(16):
            pad[r + 1, y + 1] = masked_column(vox[r, y], lo, hi, r, y)
            pad[r + 4, y + 1] = masked_column(vox[r + 5, y], lo, hi, r + 5, y)

    ends = scene_rows(((0, 0), (4, 6)), None, lo, hi, pad, w, d, cb, db, sel, cells)
    rows = (ends[0:128], inner[0:128], inner[128:256], ends[128:256])
    for pair in range(2):
        for level in range(8):
            at = slice(level * 64, level * 64 + 64)
            both = jnp.concatenate([rows[2 * pair][:, at], rows[2 * pair + 1][:, at]], axis=1)
            pieces[slots[level], :, pair * 128 : pair * 128 + 128] = both.astype(BF)
    keep[...] = pieces[0:4]
    give[...] = pieces[4:8]


def inner_rows(lo, hi, vox, ylo, yhi, tables):
    smem = pl.BlockSpec(memory_space=SMEM)
    vmem = pl.BlockSpec(memory_space=VMEM)
    return pl.pallas_call(
        inner_kernel,
        out_shape=jax.ShapeDtypeStruct((256, 512), F32),
        in_specs=[smem] * 2 + [vmem] * 8,
        out_specs=vmem,
        scratch_shapes=[VMEM((6, 18, 64, 128), BF), VMEM((256, 1024), BF)],
        compiler_params=small_vmem(12),
        cost_estimate=pl.CostEstimate(flops=5 * 10**9, bytes_accessed=4 * 10**6, transcendentals=0),
        name="inner",
    )(lo, hi, vox, ylo, yhi, *tables)


def outer_rows(lo, hi, slots, vox, ylo, yhi, xlo, xhi, inner, tables):
    half = jax.ShapeDtypeStruct((4, 128, 256), BF)
    smem = pl.BlockSpec(memory_space=SMEM)
    vmem = pl.BlockSpec(memory_space=VMEM)
    return pl.pallas_call(
        outer_kernel,
        out_shape=(half, half),
        in_specs=[smem] * 3 + [vmem] * 11,
        out_specs=(vmem, vmem),
        scratch_shapes=[
            VMEM((8, 18, 64, 128), BF),
            VMEM((256, 1024), BF),
            VMEM((8, 128, 256), BF),
        ],
        compiler_params=small_vmem(12),
        name="outer",
    )(lo, hi, slots, vox, ylo, yhi, xlo, xhi, inner, *tables)


def ring(count, step):
    return [(i, step(i) % count) for i in range(count)]


def local(voxels, shell_lo, shell_hi, conv_weight, conv_bias, down_weight, down_bias, coarse_owner):
    blk_n = lax.axis_size("blk")
    grp_n = lax.axis_size("grp")
    me = lax.axis_index("blk")
    core = me % 2

    up = [(i, i + 1) for i in range(grp_n - 1)]
    down = [(b, a) for a, b in up]
    y_first, y_last, x_first, x_last = faces(shell_lo, shell_hi, voxels)
    ylo = lax.ppermute(y_last, "grp", up)
    yhi = lax.ppermute(y_first, "grp", down)
    tables = prep(conv_weight, conv_bias, down_weight, down_bias)
    ylo, yhi, tables = lax.optimization_barrier((ylo, yhi, tables))

    ahead = [(i, i + 1) for i in range(blk_n - 1)]
    behind = [(b, a) for a, b in ahead]
    xlo = lax.ppermute(jnp.concatenate([ylo[7:8], x_last, yhi[7:8]]), "blk", ahead)
    xhi = lax.ppermute(jnp.concatenate([ylo[0:1], x_first, yhi[0:1]]), "blk", behind)
    inner = inner_rows(shell_lo, shell_hi, voxels, ylo, yhi, tables)

    column = me // 2
    owners = lax.dynamic_index_in_dim(coarse_owner[:, 0, :], column, 0, keepdims=False)
    offset = (owners - 2 * column + 3) % blk_n
    slots = (offset + 4 * core) % 8

    keep, give = outer_rows(
        shell_lo, shell_hi, slots, voxels, ylo, yhi, xlo, xhi, inner, tables
    )
    got = lax.ppermute(give, "blk", ring(blk_n, lambda i: i ^ 1))
    even = core == 0
    whole = jnp.where(
        even, jnp.concatenate([keep, got], axis=2), jnp.concatenate([got, keep], axis=2)
    )

    def mine(a, b):
        return jnp.where(even, whole[a], whole[b])

    one = lax.ppermute(mine(2, 1), "blk", ring(blk_n, lambda i: i + 1 if i % 2 else i - 1))
    two = lax.ppermute(mine(1, 2), "blk", ring(blk_n, lambda i: i + 2 if i % 2 else i - 2))
    three = lax.ppermute(mine(0, 3), "blk", ring(blk_n, lambda i: i + 3 if i % 2 else i - 3))
    stay = mine(3, 0)
    result = jnp.where(
        even, jnp.stack([three, one, stay, two]), jnp.stack([two, stay, one, three])
    )
    return result[None, None]


def solution(mesh):
    placed = (
        P("blk", "grp", None, None),
        P("blk", "grp"),
        P("blk", "grp"),
        P(),
        P(),
        P(),
        P(),
        P(None, "grp", None),
    )
    return jax.shard_map(
        local,
        mesh=mesh,
        in_specs=placed,
        out_specs=P("blk", "grp", None, None, None),
        check_vma=False,
    )
```

```python
import jax
import jax.numpy as jnp
from jax import lax
from jax.experimental import pallas as pl
from jax.experimental.pallas import tpu as pltpu
from jax.sharding import PartitionSpec as P


BF = jnp.bfloat16
F32 = jnp.float32
VMEM = pltpu.VMEM
SMEM = pltpu.SMEM


def small_vmem(mib):
    return pltpu.CompilerParams(vmem_limit_bytes=mib * 1024 * 1024)


def prep_kernel(cw, cb, dw, db, w_out, d_out, cb_out, db_out, sel_out):
    zero = jnp.zeros((64, 64), F32)
    for dx in range(3):
        for dz in range(3):
            taps = [cw[dx, dy, dz].astype(F32) for dy in range(3)]
            for yo in range(2):
                line = ([zero] if yo else []) + taps + ([] if yo else [zero])
                for half in range(2):
                    pair = jnp.concatenate(line[2 * half : 2 * half + 2], axis=0)
                    row = (dz * 2 + yo) * 64
                    col = (dx * 4 + half * 2) * 64
                    w_out[row : row + 64, col : col + 128] = pair.T.astype(BF)
    for k in range(2):
        for i in range(2):
            pair = jnp.concatenate([dw[4 * i + k], dw[4 * i + 2 + k]], axis=0).astype(F32)
            d_out[k * 128 : k * 128 + 128, i * 128 : i * 128 + 128] = pair.T.astype(BF)
    cb_out[...] = jnp.broadcast_to(cb[...], (128, 128)).T
    db_out[...] = jnp.broadcast_to(db[...], (128, 128)).T
    for q in range(8):
        z = lax.broadcasted_iota(jnp.int32, (128, 512), 0)
        lane = lax.broadcasted_iota(jnp.int32, (128, 512), 1)
        want = jnp.where(((lane >> 3) & 7) == q, 16 * (lane >> 6) + 2 * (lane & 7), -1)
        sel_out[q * 128 : q * 128 + 128, :] = jnp.where(z == want, 1.0, 0.0).astype(BF)


def prep(conv_weight, conv_bias, down_weight, down_bias):
    return pl.pallas_call(
        prep_kernel,
        out_shape=(
            jax.ShapeDtypeStruct((384, 768), BF),
            jax.ShapeDtypeStruct((256, 256), BF),
            jax.ShapeDtypeStruct((128, 128), F32),
            jax.ShapeDtypeStruct((128, 128), F32),
            jax.ShapeDtypeStruct((1024, 512), BF),
        ),
        compiler_params=small_vmem(8),
        cost_estimate=pl.CostEstimate(flops=10**9, bytes_accessed=4 * 10**6, transcendentals=0),
        name="prep",
    )(
        conv_weight,
        jnp.tile(conv_bias, 2)[None],
        down_weight,
        down_bias[None],
    )


def occupancy(lo, hi, x, y):
    lane = lax.broadcasted_iota(jnp.int32, (8, 128), 1)
    return jnp.where((lane >= lo[x, y]) & (lane < hi[x, y]), 1.0, 0.0)


def masked_column(column, lo, hi, x, y):
    mask = jnp.concatenate([occupancy(lo, hi, x, y)] * 2, axis=0).astype(BF)
    return (column.reshape(4, 16, 128) * mask[None]).reshape(64, 128)


def faces_kernel(lo, hi, vox, y_first, y_last, x_first, x_last, sems):
    copies = [
        pltpu.make_async_copy(vox.at[:, 0], y_first, sems.at[0]),
        pltpu.make_async_copy(vox.at[:, 15], y_last, sems.at[1]),
        pltpu.make_async_copy(vox.at[0], x_first, sems.at[2]),
        pltpu.make_async_copy(vox.at[7], x_last, sems.at[3]),
    ]
    for copy in copies:
        copy.start()
    for copy, ref, y in ((copies[0], y_first, 0), (copies[1], y_last, 15)):
        copy.wait()
        for x in range(8):
            ref[x] = masked_column(ref[x], lo, hi, x, y)
    for copy, ref, x in ((copies[2], x_first, 0), (copies[3], x_last, 7)):
        copy.wait()
        for y in range(16):
            ref[y] = masked_column(ref[y], lo, hi, x, y)


def faces(lo, hi, vox):
    y_face = jax.ShapeDtypeStruct((8, 64, 128), BF)
    x_face = jax.ShapeDtypeStruct((16, 64, 128), BF)
    smem = pl.BlockSpec(memory_space=SMEM)
    vmem = pl.BlockSpec(memory_space=VMEM)
    return pl.pallas_call(
        faces_kernel,
        out_shape=(y_face, y_face, x_face, x_face),
        in_specs=[smem, smem, pl.BlockSpec(memory_space=pltpu.HBM)],
        out_specs=(vmem,) * 4,
        scratch_shapes=[pltpu.SemaphoreType.DMA((4,))],
        compiler_params=small_vmem(4),
        name="faces",
    )(*(pltpu.with_memory_space_constraint(a, pltpu.HBM) for a in (lo, hi, vox)))


def scene_rows(starts, lo, hi, pad, w, d, cb, db, sel, cells):
    lane8 = lax.broadcasted_iota(jnp.int32, (8, 128), 1)
    lane = lax.broadcasted_iota(jnp.int32, (128, 128), 1)

    def conv_cell(row, x, yp):
        rows = [pad[row + r, pl.ds(2 * yp, 4)].reshape(256, 128) for r in range(4)]
        window = jnp.concatenate(
            [jnp.concatenate([rows[t], rows[t + 1]], axis=1) for t in range(3)], axis=0
        )
        summed = jnp.dot(w[...], window, preferred_element_type=F32)
        parts = []
        for xi in range(2):
            part = summed[:, xi * 128 : xi * 128 + 128]
            below = jnp.where(lane == 0, 0.0, pltpu.roll(part[0:128], 1, 1))
            above = jnp.where(lane == 127, 0.0, pltpu.roll(part[256:384], 127, 1))
            half = (below + above + part[128:256] + cb[...]) * 0.5
            act = half + half * jnp.tanh(half)
            masks = [occupancy(lo, hi, x + xi, 2 * yp + yo) for yo in range(2)]
            act = act.reshape(2, 8, 8, 128) * jnp.stack(masks)[:, None]
            parts.append(act.reshape(128, 128).astype(BF))
        return jnp.concatenate(parts, axis=0)

    def coarse_mask(x0, yp):
        found = None
        for xi in range(2):
            for yo in range(2):
                x, y = x0 + xi, 2 * yp + yo
                here = (lane8 + 1 >= lo[x, y]) & (lane8 < hi[x, y])
                found = here if found is None else found | here
        return jnp.where(found, 1.0, 0.0)

    (row0, x0), (row1, x1) = starts

    @pl.loop(0, 2)
    def _(t):
        row = row0 + t * (row1 - row0)
        x = x0 + t * (x1 - x0)
        for ypp in range(4):
            hidden = jnp.concatenate(
                [conv_cell(row, x, 2 * ypp), conv_cell(row, x, 2 * ypp + 1)], axis=1
            )
            down = jnp.dot(d[...], hidden, preferred_element_type=F32)
            for e in range(2):
                q = 2 * ypp + e
                part = down[:, e * 128 : e * 128 + 128]
                total = part[0:128] + pltpu.roll(part[128:256], 127, 1) + db[...]
                total = total.reshape(16, 8, 128) * coarse_mask(x, q)[None]
                cells[pl.ds(t * 128, 128), q * 128 : q * 128 + 128] = total.reshape(
                    128, 128
                ).astype(BF)

    return jnp.dot(cells[...], sel[...], preferred_element_type=F32)


def inner_kernel(lo, hi, vox, ylo, yhi, w, d, cb, db, sel, out, pad, cells):
    for r in range(6):
        pad[r, 0] = ylo[r + 1]
        pad[r, 17] = yhi[r + 1]

    @pl.loop(0, 6)
    def _(r):
        for y in range(16):
            pad[r, y + 1] = masked_column(vox[r + 1, y], lo, hi, r + 1, y)

    out[...] = scene_rows(((0, 2), (2, 4)), lo, hi, pad, w, d, cb, db, sel, cells)


def outer_kernel(
    lo, hi, slots, vox, ylo, yhi, xlo, xhi, inner, w, d, cb, db, sel, keep, give, pad, cells, pieces
):
    pad[0] = xlo[...]
    pad[7] = xhi[...]
    for r in range(3):
        pad[r + 1, 0] = ylo[r]
        pad[r + 1, 17] = yhi[r]
        pad[r + 4, 0] = ylo[r + 5]
        pad[r + 4, 17] = yhi[r + 5]

    @pl.loop(0, 3)
    def _(r):
        for y in range(16):
            pad[r + 1, y + 1] = masked_column(vox[r, y], lo, hi, r, y)
            pad[r + 4, y + 1] = masked_column(vox[r + 5, y], lo, hi, r + 5, y)

    ends = scene_rows(((0, 0), (4, 6)), lo, hi, pad, w, d, cb, db, sel, cells)
    rows = (ends[0:128], inner[0:128], inner[128:256], ends[128:256])
    for pair in range(2):
        for level in range(8):
            at = slice(level * 64, level * 64 + 64)
            both = jnp.concatenate([rows[2 * pair][:, at], rows[2 * pair + 1][:, at]], axis=1)
            pieces[slots[level], :, pair * 128 : pair * 128 + 128] = both.astype(BF)
    keep[...] = pieces[0:4]
    give[...] = pieces[4:8]


def inner_rows(lo, hi, vox, ylo, yhi, tables):
    smem = pl.BlockSpec(memory_space=SMEM)
    vmem = pl.BlockSpec(memory_space=VMEM)
    return pl.pallas_call(
        inner_kernel,
        out_shape=jax.ShapeDtypeStruct((256, 512), F32),
        in_specs=[smem] * 2 + [vmem] * 8,
        out_specs=vmem,
        scratch_shapes=[VMEM((6, 18, 64, 128), BF), VMEM((256, 1024), BF)],
        compiler_params=small_vmem(12),
        cost_estimate=pl.CostEstimate(flops=5 * 10**9, bytes_accessed=4 * 10**6, transcendentals=0),
        name="inner",
    )(lo, hi, vox, ylo, yhi, *tables)


def outer_rows(lo, hi, slots, vox, ylo, yhi, xlo, xhi, inner, tables):
    half = jax.ShapeDtypeStruct((4, 128, 256), BF)
    smem = pl.BlockSpec(memory_space=SMEM)
    vmem = pl.BlockSpec(memory_space=VMEM)
    return pl.pallas_call(
        outer_kernel,
        out_shape=(half, half),
        in_specs=[smem] * 3 + [vmem] * 11,
        out_specs=(vmem, vmem),
        scratch_shapes=[
            VMEM((8, 18, 64, 128), BF),
            VMEM((256, 1024), BF),
            VMEM((8, 128, 256), BF),
        ],
        compiler_params=small_vmem(12),
        name="outer",
    )(lo, hi, slots, vox, ylo, yhi, xlo, xhi, inner, *tables)


def ring(count, step):
    return [(i, step(i) % count) for i in range(count)]


def local(voxels, shell_lo, shell_hi, conv_weight, conv_bias, down_weight, down_bias, coarse_owner):
    blk_n = lax.axis_size("blk")
    grp_n = lax.axis_size("grp")
    me = lax.axis_index("blk")
    core = me % 2

    up = [(i, i + 1) for i in range(grp_n - 1)]
    down = [(b, a) for a, b in up]
    y_first, y_last, x_first, x_last = faces(shell_lo, shell_hi, voxels)
    ylo = lax.ppermute(y_last, "grp", up)
    yhi = lax.ppermute(y_first, "grp", down)
    tables = prep(conv_weight, conv_bias, down_weight, down_bias)
    ylo, yhi, tables = lax.optimization_barrier((ylo, yhi, tables))

    ahead = [(i, i + 1) for i in range(blk_n - 1)]
    behind = [(b, a) for a, b in ahead]
    xlo = lax.ppermute(jnp.concatenate([ylo[7:8], x_last, yhi[7:8]]), "blk", ahead)
    xhi = lax.ppermute(jnp.concatenate([ylo[0:1], x_first, yhi[0:1]]), "blk", behind)
    inner = inner_rows(shell_lo, shell_hi, voxels, ylo, yhi, tables)

    column = me // 2
    owners = lax.dynamic_index_in_dim(coarse_owner[:, 0, :], column, 0, keepdims=False)
    offset = (owners - 2 * column + 3) % blk_n
    ends = (offset == 0) | (offset == 7)
    offset = jnp.where(ends & (column == 0), 7 - offset, offset)
    slots = (offset + 4 * core) % 8

    keep, give = outer_rows(
        shell_lo, shell_hi, slots, voxels, ylo, yhi, xlo, xhi, inner, tables
    )
    got = lax.ppermute(give, "blk", ring(blk_n, lambda i: i ^ 1))
    even = core == 0
    whole = jnp.where(
        even, jnp.concatenate([keep, got], axis=2), jnp.concatenate([got, keep], axis=2)
    )

    def mine(a, b):
        return jnp.where(even, whole[a], whole[b])

    p_one, p_two, p_three, stay = mine(2, 1), mine(1, 2), mine(0, 3), mine(3, 0)
    odds = range(1, blk_n, 2)
    evens = range(0, blk_n, 2)
    three_pairs = [(i, (i + 3) % blk_n) for i in odds if i > 1]
    three_pairs += [(i, i - 3) for i in evens if i >= 4] + [(0, 4)]
    two_pairs = [(i, (i + 2) % blk_n) for i in odds] + [(i, i - 2) for i in evens if i >= 2]
    one_pairs = ring(blk_n, lambda i: i + 1 if i % 2 else i - 1)
    rest_pairs = [(0, blk_n - 2), (1, blk_n - 3), (2, blk_n - 1)]
    three = lax.ppermute(p_three, "blk", three_pairs)
    two = lax.ppermute(p_two, "blk", two_pairs)
    one = lax.ppermute(p_one, "blk", one_pairs)
    rest = lax.ppermute(jnp.where(me == 0, p_two, p_three), "blk", rest_pairs)
    three = jnp.where((me == blk_n - 1) | (me == blk_n - 3), rest, three)
    two = jnp.where(me == blk_n - 2, rest, two)
    result = jnp.where(
        even, jnp.stack([three, one, stay, two]), jnp.stack([two, stay, one, three])
    )
    return result[None, None]


def solution(mesh):
    placed = (
        P("blk", "grp", None, None),
        P("blk", "grp"),
        P("blk", "grp"),
        P(),
        P(),
        P(),
        P(),
        P(None, "grp", None),
    )
    return jax.shard_map(
        local,
        mesh=mesh,
        in_specs=placed,
        out_specs=P("blk", "grp", None, None, None),
        check_vma=False,
    )
```

```python
import jax
import jax.numpy as jnp
from jax import lax
from jax.experimental import pallas as pl
from jax.experimental.pallas import tpu as pltpu
from jax.sharding import PartitionSpec as P


BF = jnp.bfloat16
F32 = jnp.float32
VMEM = pltpu.VMEM
SMEM = pltpu.SMEM


def small_vmem(mib):
    return pltpu.CompilerParams(vmem_limit_bytes=mib * 1024 * 1024)


def prep_kernel(cw, cb, dw, db, w_out, d_out, cb_out, db_out, sel_out):
    zero = jnp.zeros((64, 64), F32)
    for dx in range(3):
        for dz in range(3):
            taps = [cw[dx, dy, dz].astype(F32) for dy in range(3)]
            for yo in range(2):
                line = ([zero] if yo else []) + taps + ([] if yo else [zero])
                for half in range(2):
                    pair = jnp.concatenate(line[2 * half : 2 * half + 2], axis=0)
                    row = (dz * 2 + yo) * 64
                    col = (dx * 4 + half * 2) * 64
                    w_out[row : row + 64, col : col + 128] = pair.T.astype(BF)
    for k in range(2):
        for i in range(2):
            pair = jnp.concatenate([dw[4 * i + k], dw[4 * i + 2 + k]], axis=0).astype(F32)
            d_out[k * 128 : k * 128 + 128, i * 128 : i * 128 + 128] = pair.T.astype(BF)
    cb_out[...] = jnp.broadcast_to(cb[...], (128, 128)).T
    db_out[...] = jnp.broadcast_to(db[...], (128, 128)).T
    for q in range(8):
        z = lax.broadcasted_iota(jnp.int32, (128, 512), 0)
        lane = lax.broadcasted_iota(jnp.int32, (128, 512), 1)
        want = jnp.where(((lane >> 3) & 7) == q, 16 * (lane >> 6) + 2 * (lane & 7), -1)
        sel_out[q * 128 : q * 128 + 128, :] = jnp.where(z == want, 1.0, 0.0).astype(BF)


def prep(conv_weight, conv_bias, down_weight, down_bias):
    return pl.pallas_call(
        prep_kernel,
        out_shape=(
            jax.ShapeDtypeStruct((384, 768), BF),
            jax.ShapeDtypeStruct((256, 256), BF),
            jax.ShapeDtypeStruct((128, 128), F32),
            jax.ShapeDtypeStruct((128, 128), F32),
            jax.ShapeDtypeStruct((1024, 512), BF),
        ),
        compiler_params=small_vmem(8),
        cost_estimate=pl.CostEstimate(flops=10**9, bytes_accessed=4 * 10**6, transcendentals=0),
        name="prep",
    )(
        conv_weight,
        jnp.tile(conv_bias, 2)[None],
        down_weight,
        down_bias[None],
    )


def occupancy(lo, hi, x, y):
    lane = lax.broadcasted_iota(jnp.int32, (8, 128), 1)
    return jnp.where((lane >= lo[x, y]) & (lane < hi[x, y]), 1.0, 0.0)


def masked_column(column, lo, hi, x, y):
    mask = jnp.concatenate([occupancy(lo, hi, x, y)] * 2, axis=0).astype(BF)
    return (column.reshape(4, 16, 128) * mask[None]).reshape(64, 128)


def faces_kernel(lo, hi, vox, y_first, y_last, x_first, x_last, sems):
    copies = [
        pltpu.make_async_copy(vox.at[:, 0], y_first, sems.at[0]),
        pltpu.make_async_copy(vox.at[:, 15], y_last, sems.at[1]),
        pltpu.make_async_copy(vox.at[0], x_first, sems.at[2]),
        pltpu.make_async_copy(vox.at[7], x_last, sems.at[3]),
    ]
    for copy in copies:
        copy.start()
    for copy, ref, y in ((copies[0], y_first, 0), (copies[1], y_last, 15)):
        copy.wait()
        for x in range(8):
            ref[x] = masked_column(ref[x], lo, hi, x, y)
    for copy, ref, x in ((copies[2], x_first, 0), (copies[3], x_last, 7)):
        copy.wait()
        for y in range(16):
            ref[y] = masked_column(ref[y], lo, hi, x, y)


def faces(lo, hi, vox):
    y_face = jax.ShapeDtypeStruct((8, 64, 128), BF)
    x_face = jax.ShapeDtypeStruct((16, 64, 128), BF)
    smem = pl.BlockSpec(memory_space=SMEM)
    vmem = pl.BlockSpec(memory_space=VMEM)
    return pl.pallas_call(
        faces_kernel,
        out_shape=(y_face, y_face, x_face, x_face),
        in_specs=[smem, smem, pl.BlockSpec(memory_space=pltpu.HBM)],
        out_specs=(vmem,) * 4,
        scratch_shapes=[pltpu.SemaphoreType.DMA((4,))],
        compiler_params=small_vmem(4),
        name="faces",
    )(*(pltpu.with_memory_space_constraint(a, pltpu.HBM) for a in (lo, hi, vox)))


def scene_rows(starts, lo, hi, pad, w, d, cb, db, sel, cells):
    lane8 = lax.broadcasted_iota(jnp.int32, (8, 128), 1)
    lane = lax.broadcasted_iota(jnp.int32, (128, 128), 1)

    def conv_cell(row, x, yp):
        rows = [pad[row + r, pl.ds(2 * yp, 4)].reshape(256, 128) for r in range(4)]
        window = jnp.concatenate(
            [jnp.concatenate([rows[t], rows[t + 1]], axis=1) for t in range(3)], axis=0
        )
        summed = jnp.dot(w[...], window, preferred_element_type=F32)
        parts = []
        for xi in range(2):
            part = summed[:, xi * 128 : xi * 128 + 128]
            below = jnp.where(lane == 0, 0.0, pltpu.roll(part[0:128], 1, 1))
            above = jnp.where(lane == 127, 0.0, pltpu.roll(part[256:384], 127, 1))
            half = (below + above + part[128:256] + cb[...]) * 0.5
            act = half + half * jnp.tanh(half)
            masks = [occupancy(lo, hi, x + xi, 2 * yp + yo) for yo in range(2)]
            act = act.reshape(2, 8, 8, 128) * jnp.stack(masks)[:, None]
            parts.append(act.reshape(128, 128).astype(BF))
        return jnp.concatenate(parts, axis=0)

    def coarse_mask(x0, yp):
        found = None
        for xi in range(2):
            for yo in range(2):
                x, y = x0 + xi, 2 * yp + yo
                here = (lane8 + 1 >= lo[x, y]) & (lane8 < hi[x, y])
                found = here if found is None else found | here
        return jnp.where(found, 1.0, 0.0)

    (row0, x0), (row1, x1) = starts

    for t in range(2):
        row = row0 + t * (row1 - row0)
        x = x0 + t * (x1 - x0)
        for ypp in range(4):
            hidden = jnp.concatenate(
                [conv_cell(row, x, 2 * ypp), conv_cell(row, x, 2 * ypp + 1)], axis=1
            )
            down = jnp.dot(d[...], hidden, preferred_element_type=F32)
            for e in range(2):
                q = 2 * ypp + e
                part = down[:, e * 128 : e * 128 + 128]
                total = part[0:128] + pltpu.roll(part[128:256], 127, 1) + db[...]
                total = total.reshape(16, 8, 128) * coarse_mask(x, q)[None]
                cells[t * 128 : t * 128 + 128, q * 128 : q * 128 + 128] = total.reshape(
                    128, 128
                ).astype(BF)

    return jnp.dot(cells[...], sel[...], preferred_element_type=F32)


def inner_kernel(lo, hi, vox, ylo, yhi, w, d, cb, db, sel, out, pad, cells):
    for r in range(6):
        pad[r, 0] = ylo[r + 1]
        pad[r, 17] = yhi[r + 1]

    @pl.loop(0, 6)
    def _(r):
        for y in range(16):
            pad[r, y + 1] = masked_column(vox[r + 1, y], lo, hi, r + 1, y)

    out[...] = scene_rows(((0, 2), (2, 4)), lo, hi, pad, w, d, cb, db, sel, cells)


def outer_kernel(
    lo, hi, slots, vox, ylo, yhi, xlo, xhi, inner, w, d, cb, db, sel, keep, give, pad, cells, pieces
):
    pad[0] = xlo[...]
    pad[7] = xhi[...]
    for r in range(3):
        pad[r + 1, 0] = ylo[r]
        pad[r + 1, 17] = yhi[r]
        pad[r + 4, 0] = ylo[r + 5]
        pad[r + 4, 17] = yhi[r + 5]

    @pl.loop(0, 3)
    def _(r):
        for y in range(16):
            pad[r + 1, y + 1] = masked_column(vox[r, y], lo, hi, r, y)
            pad[r + 4, y + 1] = masked_column(vox[r + 5, y], lo, hi, r + 5, y)

    ends = scene_rows(((0, 0), (4, 6)), lo, hi, pad, w, d, cb, db, sel, cells)
    rows = (ends[0:128], inner[0:128], inner[128:256], ends[128:256])
    for pair in range(2):
        for level in range(8):
            at = slice(level * 64, level * 64 + 64)
            both = jnp.concatenate([rows[2 * pair][:, at], rows[2 * pair + 1][:, at]], axis=1)
            pieces[slots[level], :, pair * 128 : pair * 128 + 128] = both.astype(BF)
    keep[...] = pieces[0:4]
    give[...] = pieces[4:8]


def inner_rows(lo, hi, vox, ylo, yhi, tables):
    smem = pl.BlockSpec(memory_space=SMEM)
    vmem = pl.BlockSpec(memory_space=VMEM)
    return pl.pallas_call(
        inner_kernel,
        out_shape=jax.ShapeDtypeStruct((256, 512), F32),
        in_specs=[smem] * 2 + [vmem] * 8,
        out_specs=vmem,
        scratch_shapes=[VMEM((6, 18, 64, 128), BF), VMEM((256, 1024), BF)],
        compiler_params=small_vmem(12),
        cost_estimate=pl.CostEstimate(flops=5 * 10**9, bytes_accessed=4 * 10**6, transcendentals=0),
        name="inner",
    )(lo, hi, vox, ylo, yhi, *tables)


def outer_rows(lo, hi, slots, vox, ylo, yhi, xlo, xhi, inner, tables):
    half = jax.ShapeDtypeStruct((4, 128, 256), BF)
    smem = pl.BlockSpec(memory_space=SMEM)
    vmem = pl.BlockSpec(memory_space=VMEM)
    return pl.pallas_call(
        outer_kernel,
        out_shape=(half, half),
        in_specs=[smem] * 3 + [vmem] * 11,
        out_specs=(vmem, vmem),
        scratch_shapes=[
            VMEM((8, 18, 64, 128), BF),
            VMEM((256, 1024), BF),
            VMEM((8, 128, 256), BF),
        ],
        compiler_params=small_vmem(12),
        name="outer",
    )(lo, hi, slots, vox, ylo, yhi, xlo, xhi, inner, *tables)


def ring(count, step):
    return [(i, step(i) % count) for i in range(count)]


def local(voxels, shell_lo, shell_hi, conv_weight, conv_bias, down_weight, down_bias, coarse_owner):
    blk_n = lax.axis_size("blk")
    grp_n = lax.axis_size("grp")
    me = lax.axis_index("blk")
    core = me % 2

    up = [(i, i + 1) for i in range(grp_n - 1)]
    down = [(b, a) for a, b in up]
    y_first, y_last, x_first, x_last = faces(shell_lo, shell_hi, voxels)
    ylo = lax.ppermute(y_last, "grp", up)
    yhi = lax.ppermute(y_first, "grp", down)
    tables = prep(conv_weight, conv_bias, down_weight, down_bias)
    ylo, yhi, tables = lax.optimization_barrier((ylo, yhi, tables))

    ahead = [(i, i + 1) for i in range(blk_n - 1)]
    behind = [(b, a) for a, b in ahead]
    xlo = lax.ppermute(jnp.concatenate([ylo[7:8], x_last, yhi[7:8]]), "blk", ahead)
    xhi = lax.ppermute(jnp.concatenate([ylo[0:1], x_first, yhi[0:1]]), "blk", behind)
    inner = inner_rows(shell_lo, shell_hi, voxels, ylo, yhi, tables)

    column = me // 2
    owners = lax.dynamic_index_in_dim(coarse_owner[:, 0, :], column, 0, keepdims=False)
    offset = (owners - 2 * column + 3) % blk_n
    slots = (offset + 4 * core) % 8

    keep, give = outer_rows(
        shell_lo, shell_hi, slots, voxels, ylo, yhi, xlo, xhi, inner, tables
    )
    got = lax.ppermute(give, "blk", ring(blk_n, lambda i: i ^ 1))
    even = core == 0
    whole = jnp.where(
        even, jnp.concatenate([keep, got], axis=2), jnp.concatenate([got, keep], axis=2)
    )

    def mine(a, b):
        return jnp.where(even, whole[a], whole[b])

    pairs = ring(blk_n, lambda i: i + 1 if i % 2 else i - 1)
    one = lax.ppermute(mine(2, 1), "blk", pairs)
    pairs = ring(blk_n, lambda i: i + 3 if i % 2 else i - 3)
    three = lax.ppermute(mine(0, 3), "blk", pairs)
    pairs = ring(blk_n, lambda i: i + 2 if i % 2 else i - 2)
    two = lax.ppermute(mine(1, 2), "blk", pairs)
    stay = mine(3, 0)
    result = jnp.where(
        even, jnp.stack([three, one, stay, two]), jnp.stack([two, stay, one, three])
    )
    return result[None, None]


def solution(mesh):
    placed = (
        P("blk", "grp", None, None),
        P("blk", "grp"),
        P("blk", "grp"),
        P(),
        P(),
        P(),
        P(),
        P(None, "grp", None),
    )
    return jax.shard_map(
        local,
        mesh=mesh,
        in_specs=placed,
        out_specs=P("blk", "grp", None, None, None),
        check_vma=False,
    )
```

```python
import jax
import jax.numpy as jnp
from jax import lax
from jax.experimental import pallas as pl
from jax.experimental.pallas import tpu as pltpu
from jax.sharding import PartitionSpec as P


BF = jnp.bfloat16
F32 = jnp.float32
VMEM = pltpu.VMEM
SMEM = pltpu.SMEM


def small_vmem(mib):
    return pltpu.CompilerParams(vmem_limit_bytes=mib * 1024 * 1024)


def prep_kernel(cw, cb, dw, db, w_out, d_out, cb_out, db_out, sel_out):
    zero = jnp.zeros((64, 64), F32)
    for dx in range(3):
        for dz in range(3):
            taps = [cw[dx, dy, dz].astype(F32) for dy in range(3)]
            for yo in range(2):
                line = ([zero] if yo else []) + taps + ([] if yo else [zero])
                for half in range(2):
                    pair = jnp.concatenate(line[2 * half : 2 * half + 2], axis=0)
                    row = (dz * 2 + yo) * 64
                    col = (dx * 4 + half * 2) * 64
                    w_out[row : row + 64, col : col + 128] = pair.T.astype(BF)
    for k in range(2):
        for i in range(2):
            pair = jnp.concatenate([dw[4 * i + k], dw[4 * i + 2 + k]], axis=0).astype(F32)
            d_out[k * 128 : k * 128 + 128, i * 128 : i * 128 + 128] = pair.T.astype(BF)
    cb_out[...] = jnp.broadcast_to(cb[...], (128, 128)).T
    db_out[...] = jnp.broadcast_to(db[...], (128, 128)).T
    for q in range(8):
        z = lax.broadcasted_iota(jnp.int32, (128, 512), 0)
        lane = lax.broadcasted_iota(jnp.int32, (128, 512), 1)
        want = jnp.where(((lane >> 3) & 7) == q, 16 * (lane >> 6) + 2 * (lane & 7), -1)
        sel_out[q * 128 : q * 128 + 128, :] = jnp.where(z == want, 1.0, 0.0).astype(BF)


def prep(conv_weight, conv_bias, down_weight, down_bias):
    return pl.pallas_call(
        prep_kernel,
        out_shape=(
            jax.ShapeDtypeStruct((384, 768), BF),
            jax.ShapeDtypeStruct((256, 256), BF),
            jax.ShapeDtypeStruct((128, 128), F32),
            jax.ShapeDtypeStruct((128, 128), F32),
            jax.ShapeDtypeStruct((1024, 512), BF),
        ),
        compiler_params=small_vmem(8),
        cost_estimate=pl.CostEstimate(flops=10**9, bytes_accessed=4 * 10**6, transcendentals=0),
        name="prep",
    )(
        conv_weight,
        jnp.tile(conv_bias, 2)[None],
        down_weight,
        down_bias[None],
    )


def occupancy(lo, hi, x, y):
    lane = lax.broadcasted_iota(jnp.int32, (8, 128), 1)
    return jnp.where((lane >= lo[x, y]) & (lane < hi[x, y]), 1.0, 0.0)


def masked_column(column, lo, hi, x, y):
    mask = jnp.concatenate([occupancy(lo, hi, x, y)] * 2, axis=0).astype(BF)
    return (column.reshape(4, 16, 128) * mask[None]).reshape(64, 128)


def faces_kernel(side, lo, hi, vox, y_one, y_two, x_one, x_two, sems):
    core, odd = side[0] & 1, side[0] >> 1
    y_at = (jnp.where(odd == 1, 0, 15), jnp.where(odd == 1, 15, 0))
    x_at = (jnp.where(core == 1, 0, 7), jnp.where(core == 1, 7, 0))
    y_copies = [
        pltpu.make_async_copy(vox.at[:, y_at[k]], ref, sems.at[k])
        for k, ref in enumerate((y_one, y_two))
    ]
    x_copies = [
        pltpu.make_async_copy(vox.at[x_at[k]], ref, sems.at[2 + k])
        for k, ref in enumerate((x_one, x_two))
    ]
    for copy in y_copies + x_copies:
        copy.start()
    for copy, ref, y in zip(y_copies, (y_one, y_two), y_at):
        copy.wait()
        for x in range(8):
            ref[x] = masked_column(ref[x], lo, hi, x, y)
    for copy, ref, x in zip(x_copies, (x_one, x_two), x_at):
        copy.wait()
        for y in range(16):
            ref[y] = masked_column(ref[y], lo, hi, x, y)


def faces(side, lo, hi, vox):
    y_face = jax.ShapeDtypeStruct((8, 64, 128), BF)
    x_face = jax.ShapeDtypeStruct((16, 64, 128), BF)
    smem = pl.BlockSpec(memory_space=SMEM)
    vmem = pl.BlockSpec(memory_space=VMEM)
    return pl.pallas_call(
        faces_kernel,
        out_shape=(y_face, y_face, x_face, x_face),
        in_specs=[smem] * 3 + [pl.BlockSpec(memory_space=pltpu.HBM)],
        out_specs=(vmem,) * 4,
        scratch_shapes=[pltpu.SemaphoreType.DMA((4,))],
        compiler_params=small_vmem(4),
        name="faces",
    )(side, *(pltpu.with_memory_space_constraint(a, pltpu.HBM) for a in (lo, hi, vox)))


def scene_rows(starts, lo, hi, pad, w, d, cb, db, sel, cells):
    lane8 = lax.broadcasted_iota(jnp.int32, (8, 128), 1)
    lane = lax.broadcasted_iota(jnp.int32, (128, 128), 1)

    def conv_cell(row, x, yp):
        rows = [pad[row + r, pl.ds(2 * yp, 4)].reshape(256, 128) for r in range(4)]
        window = jnp.concatenate(
            [jnp.concatenate([rows[t], rows[t + 1]], axis=1) for t in range(3)], axis=0
        )
        summed = jnp.dot(w[...], window, preferred_element_type=F32)
        parts = []
        for xi in range(2):
            part = summed[:, xi * 128 : xi * 128 + 128]
            below = jnp.where(lane == 0, 0.0, pltpu.roll(part[0:128], 1, 1))
            above = jnp.where(lane == 127, 0.0, pltpu.roll(part[256:384], 127, 1))
            half = (below + above + part[128:256] + cb[...]) * 0.5
            act = half + half * jnp.tanh(half)
            masks = [occupancy(lo, hi, x + xi, 2 * yp + yo) for yo in range(2)]
            act = act.reshape(2, 8, 8, 128) * jnp.stack(masks)[:, None]
            parts.append(act.reshape(128, 128).astype(BF))
        return jnp.concatenate(parts, axis=0)

    def coarse_mask(x0, yp):
        found = None
        for xi in range(2):
            for yo in range(2):
                x, y = x0 + xi, 2 * yp + yo
                here = (lane8 + 1 >= lo[x, y]) & (lane8 < hi[x, y])
                found = here if found is None else found | here
        return jnp.where(found, 1.0, 0.0)

    (row0, x0), (row1, x1) = starts

    for t in range(2):
        row = row0 + t * (row1 - row0)
        x = x0 + t * (x1 - x0)
        for ypp in range(4):
            hidden = jnp.concatenate(
                [conv_cell(row, x, 2 * ypp), conv_cell(row, x, 2 * ypp + 1)], axis=1
            )
            down = jnp.dot(d[...], hidden, preferred_element_type=F32)
            for e in range(2):
                q = 2 * ypp + e
                part = down[:, e * 128 : e * 128 + 128]
                total = part[0:128] + pltpu.roll(part[128:256], 127, 1) + db[...]
                total = total.reshape(16, 8, 128) * coarse_mask(x, q)[None]
                cells[t * 128 : t * 128 + 128, q * 128 : q * 128 + 128] = total.reshape(
                    128, 128
                ).astype(BF)

    return jnp.dot(cells[...], sel[...], preferred_element_type=F32)


def inner_kernel(side, lo, hi, vox, y_one, y_two, w, d, cb, db, sel, out, pad, cells):
    odd = side[0] >> 1
    one_at, two_at = 17 * (1 - odd), 17 * odd
    for r in range(6):
        pad[r, one_at] = y_one[r + 1]
        pad[r, two_at] = y_two[r + 1]

    @pl.loop(0, 6)
    def _(r):
        for y in range(16):
            pad[r, y + 1] = masked_column(vox[r + 1, y], lo, hi, r + 1, y)

    out[...] = scene_rows(((0, 2), (2, 4)), lo, hi, pad, w, d, cb, db, sel, cells)


def outer_kernel(
    side, lo, hi, slots, vox, y_one, y_two, x_one, x_two, inner, w, d, cb, db, sel, keep, give, pad, cells, pieces
):
    core, odd = side[0] & 1, side[0] >> 1
    one_at, two_at = 17 * (1 - odd), 17 * odd
    pad[7 * (1 - core)] = x_one[...]
    pad[7 * core] = x_two[...]
    for r in range(3):
        pad[r + 1, one_at] = y_one[r]
        pad[r + 1, two_at] = y_two[r]
        pad[r + 4, one_at] = y_one[r + 5]
        pad[r + 4, two_at] = y_two[r + 5]

    @pl.loop(0, 3)
    def _(r):
        for y in range(16):
            pad[r + 1, y + 1] = masked_column(vox[r, y], lo, hi, r, y)
            pad[r + 4, y + 1] = masked_column(vox[r + 5, y], lo, hi, r + 5, y)

    ends = scene_rows(((0, 0), (4, 6)), lo, hi, pad, w, d, cb, db, sel, cells)
    rows = (ends[0:128], inner[0:128], inner[128:256], ends[128:256])
    for pair in range(2):
        for level in range(8):
            at = slice(level * 64, level * 64 + 64)
            both = jnp.concatenate([rows[2 * pair][:, at], rows[2 * pair + 1][:, at]], axis=1)
            pieces[slots[level], :, pair * 128 : pair * 128 + 128] = both.astype(BF)
    keep[...] = pieces[0:4]
    give[...] = pieces[4:8]


def inner_rows(side, lo, hi, vox, y_one, y_two, tables):
    smem = pl.BlockSpec(memory_space=SMEM)
    vmem = pl.BlockSpec(memory_space=VMEM)
    return pl.pallas_call(
        inner_kernel,
        out_shape=jax.ShapeDtypeStruct((256, 512), F32),
        in_specs=[smem] * 3 + [vmem] * 8,
        out_specs=vmem,
        scratch_shapes=[VMEM((6, 18, 64, 128), BF), VMEM((256, 1024), BF)],
        compiler_params=small_vmem(12),
        cost_estimate=pl.CostEstimate(flops=5 * 10**9, bytes_accessed=4 * 10**6, transcendentals=0),
        name="inner",
    )(side, lo, hi, vox, y_one, y_two, *tables)


def outer_rows(side, lo, hi, slots, vox, y_one, y_two, x_one, x_two, inner, tables):
    half = jax.ShapeDtypeStruct((4, 128, 256), BF)
    smem = pl.BlockSpec(memory_space=SMEM)
    vmem = pl.BlockSpec(memory_space=VMEM)
    return pl.pallas_call(
        outer_kernel,
        out_shape=(half, half),
        in_specs=[smem] * 4 + [vmem] * 11,
        out_specs=(vmem, vmem),
        scratch_shapes=[
            VMEM((8, 18, 64, 128), BF),
            VMEM((256, 1024), BF),
            VMEM((8, 128, 256), BF),
        ],
        compiler_params=small_vmem(12),
        name="outer",
    )(side, lo, hi, slots, vox, y_one, y_two, x_one, x_two, inner, *tables)


def ring(count, step):
    return [(i, step(i) % count) for i in range(count)]


def local(voxels, shell_lo, shell_hi, conv_weight, conv_bias, down_weight, down_bias, coarse_owner):
    blk_n = lax.axis_size("blk")
    grp_n = lax.axis_size("grp")
    me = lax.axis_index("blk")
    core = me % 2

    grp_odd = lax.axis_index("grp") % 2
    side = (core + 2 * grp_odd).astype(jnp.int32).reshape(1)

    def swaps(count, first):
        lower = range(first, count - 1, 2)
        return [(i, i + 1) for i in lower] + [(i + 1, i) for i in lower]

    y_one, y_two, x_one, x_two = faces(side, shell_lo, shell_hi, voxels)
    y_one = lax.ppermute(y_one, "grp", swaps(grp_n, 0))
    y_two = lax.ppermute(y_two, "grp", swaps(grp_n, 1))
    tables = prep(conv_weight, conv_bias, down_weight, down_bias)
    y_one, y_two, tables = lax.optimization_barrier((y_one, y_two, tables))

    def x_message(face, last_row):
        ones = jnp.where(last_row, y_one[7:8], y_one[0:1])
        twos = jnp.where(last_row, y_two[7:8], y_two[0:1])
        low = jnp.where(grp_odd == 1, ones, twos)
        high = jnp.where(grp_odd == 1, twos, ones)
        return jnp.concatenate([low, face, high])

    x_one = lax.ppermute(x_message(x_one, core == 0), "blk", swaps(blk_n, 0))
    x_two = lax.ppermute(x_message(x_two, core == 1), "blk", swaps(blk_n, 1))
    inner = inner_rows(side, shell_lo, shell_hi, voxels, y_one, y_two, tables)

    column = me // 2
    owners = lax.dynamic_index_in_dim(coarse_owner[:, 0, :], column, 0, keepdims=False)
    offset = (owners - 2 * column + 3) % blk_n
    slots = (offset + 4 * core) % 8

    keep, give = outer_rows(
        side, shell_lo, shell_hi, slots, voxels, y_one, y_two, x_one, x_two, inner, tables
    )
    got = lax.ppermute(give, "blk", ring(blk_n, lambda i: i ^ 1))
    even = core == 0
    whole = jnp.where(
        even, jnp.concatenate([keep, got], axis=2), jnp.concatenate([got, keep], axis=2)
    )

    def mine(a, b):
        return jnp.where(even, whole[a], whole[b])

    pairs = ring(blk_n, lambda i: i + 1 if i % 2 else i - 1)
    one = lax.ppermute(mine(2, 1), "blk", pairs)
    pairs = ring(blk_n, lambda i: i + 3 if i % 2 else i - 3)
    three = lax.ppermute(mine(0, 3), "blk", pairs)
    pairs = ring(blk_n, lambda i: i + 2 if i % 2 else i - 2)
    two = lax.ppermute(mine(1, 2), "blk", pairs)
    stay = mine(3, 0)
    result = jnp.where(
        even, jnp.stack([three, one, stay, two]), jnp.stack([two, stay, one, three])
    )
    return result[None, None]


def solution(mesh):
    placed = (
        P("blk", "grp", None, None),
        P("blk", "grp"),
        P("blk", "grp"),
        P(),
        P(),
        P(),
        P(),
        P(None, "grp", None),
    )
    return jax.shard_map(
        local,
        mesh=mesh,
        in_specs=placed,
        out_specs=P("blk", "grp", None, None, None),
        check_vma=False,
    )
```

```python
import jax
import jax.numpy as jnp
from jax import lax
from jax.experimental import pallas as pl
from jax.experimental.pallas import tpu as pltpu
from jax.sharding import PartitionSpec as P


BF = jnp.bfloat16
F32 = jnp.float32
VMEM = pltpu.VMEM
SMEM = pltpu.SMEM


def small_vmem(mib):
    return pltpu.CompilerParams(vmem_limit_bytes=mib * 1024 * 1024)


def occupancy(lo, hi, x, y):
    lane = lax.broadcasted_iota(jnp.int32, (8, 128), 1)
    return jnp.where((lane >= lo[x, y]) & (lane < hi[x, y]), 1.0, 0.0)


def masked_column(column, lo, hi, x, y):
    mask = jnp.concatenate([occupancy(lo, hi, x, y)] * 2, axis=0).astype(BF)
    return (column.reshape(4, 16, 128) * mask[None]).reshape(64, 128)


def prep_kernel(
    side, lo, hi, vox, cw, cb, dw, db, x_one, x_two, w_out, d_out, cb_out, db_out, sel_out, sems
):
    core = side[0] & 1
    x_at = (jnp.where(core == 1, 0, 7), jnp.where(core == 1, 7, 0))
    copies = [
        pltpu.make_async_copy(vox.at[x_at[k]], ref, sems.at[k])
        for k, ref in enumerate((x_one, x_two))
    ]
    for copy in copies:
        copy.start()
    zero = jnp.zeros((64, 64), F32)
    for dx in range(3):
        for dz in range(3):
            taps = [cw[dx, dy, dz].astype(F32) for dy in range(3)]
            for yo in range(2):
                line = ([zero] if yo else []) + taps + ([] if yo else [zero])
                for half in range(2):
                    pair = jnp.concatenate(line[2 * half : 2 * half + 2], axis=0)
                    row = (dz * 2 + yo) * 64
                    col = (dx * 4 + half * 2) * 64
                    w_out[row : row + 64, col : col + 128] = pair.T.astype(BF)
    for k in range(2):
        for i in range(2):
            pair = jnp.concatenate([dw[4 * i + k], dw[4 * i + 2 + k]], axis=0).astype(F32)
            d_out[k * 128 : k * 128 + 128, i * 128 : i * 128 + 128] = pair.T.astype(BF)
    cb_out[...] = jnp.broadcast_to(cb[...], (128, 128)).T
    db_out[...] = jnp.broadcast_to(db[...], (128, 128)).T
    for q in range(8):
        z = lax.broadcasted_iota(jnp.int32, (128, 512), 0)
        lane = lax.broadcasted_iota(jnp.int32, (128, 512), 1)
        want = jnp.where(((lane >> 3) & 7) == q, 16 * (lane >> 6) + 2 * (lane & 7), -1)
        sel_out[q * 128 : q * 128 + 128, :] = jnp.where(z == want, 1.0, 0.0).astype(BF)
    for copy, ref, x in zip(copies, (x_one, x_two), x_at):
        copy.wait()
        for y in range(16):
            ref[y] = masked_column(ref[y], lo, hi, x, y)


def prep(side, lo, hi, vox, conv_weight, conv_bias, down_weight, down_bias):
    smem = pl.BlockSpec(memory_space=SMEM)
    vmem = pl.BlockSpec(memory_space=VMEM)
    x_face = jax.ShapeDtypeStruct((16, 64, 128), BF)
    return pl.pallas_call(
        prep_kernel,
        out_shape=(
            x_face,
            x_face,
            jax.ShapeDtypeStruct((384, 768), BF),
            jax.ShapeDtypeStruct((256, 256), BF),
            jax.ShapeDtypeStruct((128, 128), F32),
            jax.ShapeDtypeStruct((128, 128), F32),
            jax.ShapeDtypeStruct((1024, 512), BF),
        ),
        in_specs=[smem] * 3 + [pl.BlockSpec(memory_space=pltpu.HBM)] + [vmem] * 4,
        out_specs=(vmem,) * 7,
        scratch_shapes=[pltpu.SemaphoreType.DMA((2,))],
        compiler_params=small_vmem(8),
        cost_estimate=pl.CostEstimate(flops=10**9, bytes_accessed=4 * 10**6, transcendentals=0),
        name="prep",
    )(
        side,
        *in_place(lo, hi, vox),
        conv_weight,
        jnp.tile(conv_bias, 2)[None],
        down_weight,
        down_bias[None],
    )


def faces_kernel(side, lo, hi, vox, y_one, y_two, sems):
    odd = side[0] >> 1
    y_at = (jnp.where(odd == 1, 0, 15), jnp.where(odd == 1, 15, 0))
    copies = [
        pltpu.make_async_copy(vox.at[:, y_at[k]], ref, sems.at[k])
        for k, ref in enumerate((y_one, y_two))
    ]
    for copy in copies:
        copy.start()
    for copy, ref, y in zip(copies, (y_one, y_two), y_at):
        copy.wait()
        for x in range(8):
            ref[x] = masked_column(ref[x], lo, hi, x, y)


def in_place(*arrays):
    return tuple(pltpu.with_memory_space_constraint(a, pltpu.HBM) for a in arrays)


def faces(side, lo, hi, vox):
    y_face = jax.ShapeDtypeStruct((8, 64, 128), BF)
    smem = pl.BlockSpec(memory_space=SMEM)
    vmem = pl.BlockSpec(memory_space=VMEM)
    return pl.pallas_call(
        faces_kernel,
        out_shape=(y_face, y_face),
        in_specs=[smem] * 3 + [pl.BlockSpec(memory_space=pltpu.HBM)],
        out_specs=(vmem, vmem),
        scratch_shapes=[pltpu.SemaphoreType.DMA((2,))],
        compiler_params=small_vmem(4),
        name="faces",
    )(side, *in_place(lo, hi, vox))


def scene_rows(starts, lo, hi, pad, w, d, cb, db, sel, cells):
    lane8 = lax.broadcasted_iota(jnp.int32, (8, 128), 1)
    lane = lax.broadcasted_iota(jnp.int32, (128, 128), 1)

    def conv_cell(row, x, yp):
        rows = [pad[row + r, pl.ds(2 * yp, 4)].reshape(256, 128) for r in range(4)]
        window = jnp.concatenate(
            [jnp.concatenate([rows[t], rows[t + 1]], axis=1) for t in range(3)], axis=0
        )
        summed = jnp.dot(w[...], window, preferred_element_type=F32)
        parts = []
        for xi in range(2):
            part = summed[:, xi * 128 : xi * 128 + 128]
            below = jnp.where(lane == 0, 0.0, pltpu.roll(part[0:128], 1, 1))
            above = jnp.where(lane == 127, 0.0, pltpu.roll(part[256:384], 127, 1))
            half = (below + above + part[128:256] + cb[...]) * 0.5
            act = half + half * jnp.tanh(half)
            masks = [occupancy(lo, hi, x + xi, 2 * yp + yo) for yo in range(2)]
            act = act.reshape(2, 8, 8, 128) * jnp.stack(masks)[:, None]
            parts.append(act.reshape(128, 128).astype(BF))
        return jnp.concatenate(parts, axis=0)

    def coarse_mask(x0, yp):
        found = None
        for xi in range(2):
            for yo in range(2):
                x, y = x0 + xi, 2 * yp + yo
                here = (lane8 + 1 >= lo[x, y]) & (lane8 < hi[x, y])
                found = here if found is None else found | here
        return jnp.where(found, 1.0, 0.0)

    (row0, x0), (row1, x1) = starts

    for t in range(2):
        row = row0 + t * (row1 - row0)
        x = x0 + t * (x1 - x0)
        for ypp in range(4):
            hidden = jnp.concatenate(
                [conv_cell(row, x, 2 * ypp), conv_cell(row, x, 2 * ypp + 1)], axis=1
            )
            down = jnp.dot(d[...], hidden, preferred_element_type=F32)
            for e in range(2):
                q = 2 * ypp + e
                part = down[:, e * 128 : e * 128 + 128]
                total = part[0:128] + pltpu.roll(part[128:256], 127, 1) + db[...]
                total = total.reshape(16, 8, 128) * coarse_mask(x, q)[None]
                cells[t * 128 : t * 128 + 128, q * 128 : q * 128 + 128] = total.reshape(
                    128, 128
                ).astype(BF)

    return jnp.dot(cells[...], sel[...], preferred_element_type=F32)


def inner_kernel(side, lo, hi, vox, y_one, y_two, w, d, cb, db, sel, out, pad, cells):
    odd = side[0] >> 1
    one_at, two_at = 17 * (1 - odd), 17 * odd
    for r in range(6):
        pad[r, one_at] = y_one[r + 1]
        pad[r, two_at] = y_two[r + 1]

    @pl.loop(0, 6)
    def _(r):
        for y in range(16):
            pad[r, y + 1] = masked_column(vox[r + 1, y], lo, hi, r + 1, y)

    out[...] = scene_rows(((0, 2), (2, 4)), lo, hi, pad, w, d, cb, db, sel, cells)


def outer_kernel(
    side, lo, hi, slots, vox, y_one, y_two, x_one, x_two, inner, w, d, cb, db, sel, keep, give, pad, cells, pieces
):
    core, odd = side[0] & 1, side[0] >> 1
    one_at, two_at = 17 * (1 - odd), 17 * odd
    pad[7 * (1 - core)] = x_one[...]
    pad[7 * core] = x_two[...]
    for r in range(3):
        pad[r + 1, one_at] = y_one[r]
        pad[r + 1, two_at] = y_two[r]
        pad[r + 4, one_at] = y_one[r + 5]
        pad[r + 4, two_at] = y_two[r + 5]

    @pl.loop(0, 3)
    def _(r):
        for y in range(16):
            pad[r + 1, y + 1] = masked_column(vox[r, y], lo, hi, r, y)
            pad[r + 4, y + 1] = masked_column(vox[r + 5, y], lo, hi, r + 5, y)

    ends = scene_rows(((0, 0), (4, 6)), lo, hi, pad, w, d, cb, db, sel, cells)
    rows = (ends[0:128], inner[0:128], inner[128:256], ends[128:256])
    for pair in range(2):
        for level in range(8):
            at = slice(level * 64, level * 64 + 64)
            both = jnp.concatenate([rows[2 * pair][:, at], rows[2 * pair + 1][:, at]], axis=1)
            pieces[slots[level], :, pair * 128 : pair * 128 + 128] = both.astype(BF)
    keep[...] = pieces[0:4]
    give[...] = pieces[4:8]


def inner_rows(side, lo, hi, vox, y_one, y_two, tables):
    smem = pl.BlockSpec(memory_space=SMEM)
    vmem = pl.BlockSpec(memory_space=VMEM)
    return pl.pallas_call(
        inner_kernel,
        out_shape=jax.ShapeDtypeStruct((256, 512), F32),
        in_specs=[smem] * 3 + [vmem] * 8,
        out_specs=vmem,
        scratch_shapes=[VMEM((6, 18, 64, 128), BF), VMEM((256, 1024), BF)],
        compiler_params=small_vmem(12),
        cost_estimate=pl.CostEstimate(flops=5 * 10**9, bytes_accessed=4 * 10**6, transcendentals=0),
        name="inner",
    )(side, lo, hi, vox, y_one, y_two, *tables)


def outer_rows(side, lo, hi, slots, vox, y_one, y_two, x_one, x_two, inner, tables):
    half = jax.ShapeDtypeStruct((4, 128, 256), BF)
    smem = pl.BlockSpec(memory_space=SMEM)
    vmem = pl.BlockSpec(memory_space=VMEM)
    return pl.pallas_call(
        outer_kernel,
        out_shape=(half, half),
        in_specs=[smem] * 4 + [vmem] * 11,
        out_specs=(vmem, vmem),
        scratch_shapes=[
            VMEM((8, 18, 64, 128), BF),
            VMEM((256, 1024), BF),
            VMEM((8, 128, 256), BF),
        ],
        compiler_params=small_vmem(12),
        name="outer",
    )(side, lo, hi, slots, vox, y_one, y_two, x_one, x_two, inner, *tables)


def ring(count, step):
    return [(i, step(i) % count) for i in range(count)]


def local(voxels, shell_lo, shell_hi, conv_weight, conv_bias, down_weight, down_bias, coarse_owner):
    blk_n = lax.axis_size("blk")
    grp_n = lax.axis_size("grp")
    me = lax.axis_index("blk")
    core = me % 2

    grp_odd = lax.axis_index("grp") % 2
    side = (core + 2 * grp_odd).astype(jnp.int32).reshape(1)

    def swaps(count, first):
        lower = range(first, count - 1, 2)
        return [(i, i + 1) for i in lower] + [(i + 1, i) for i in lower]

    y_one, y_two = faces(side, shell_lo, shell_hi, voxels)
    y_one = lax.ppermute(y_one, "grp", swaps(grp_n, 0))
    y_two = lax.ppermute(y_two, "grp", swaps(grp_n, 1))
    x_one, x_two, *tables = prep(
        side, shell_lo, shell_hi, voxels, conv_weight, conv_bias, down_weight, down_bias
    )
    y_one, y_two, tables = lax.optimization_barrier((y_one, y_two, tuple(tables)))

    def x_message(face, last_row):
        ones = jnp.where(last_row, y_one[7:8], y_one[0:1])
        twos = jnp.where(last_row, y_two[7:8], y_two[0:1])
        low = jnp.where(grp_odd == 1, ones, twos)
        high = jnp.where(grp_odd == 1, twos, ones)
        return jnp.concatenate([low, face, high])

    x_one = lax.ppermute(x_message(x_one, core == 0), "blk", swaps(blk_n, 0))
    x_two = lax.ppermute(x_message(x_two, core == 1), "blk", swaps(blk_n, 1))
    inner = inner_rows(side, shell_lo, shell_hi, voxels, y_one, y_two, tables)

    column = me // 2
    owners = lax.dynamic_index_in_dim(coarse_owner[:, 0, :], column, 0, keepdims=False)
    offset = (owners - 2 * column + 3) % blk_n
    slots = (offset + 4 * core) % 8

    keep, give = outer_rows(
        side, shell_lo, shell_hi, slots, voxels, y_one, y_two, x_one, x_two, inner, tables
    )
    got = lax.ppermute(give, "blk", ring(blk_n, lambda i: i ^ 1))
    even = core == 0
    whole = jnp.where(
        even, jnp.concatenate([keep, got], axis=2), jnp.concatenate([got, keep], axis=2)
    )

    def mine(a, b):
        return jnp.where(even, whole[a], whole[b])

    pairs = ring(blk_n, lambda i: i + 1 if i % 2 else i - 1)
    one = lax.ppermute(mine(2, 1), "blk", pairs)
    pairs = ring(blk_n, lambda i: i + 3 if i % 2 else i - 3)
    three = lax.ppermute(mine(0, 3), "blk", pairs)
    pairs = ring(blk_n, lambda i: i + 2 if i % 2 else i - 2)
    two = lax.ppermute(mine(1, 2), "blk", pairs)
    stay = mine(3, 0)
    result = jnp.where(
        even, jnp.stack([three, one, stay, two]), jnp.stack([two, stay, one, three])
    )
    return result[None, None]


def solution(mesh):
    placed = (
        P("blk", "grp", None, None),
        P("blk", "grp"),
        P("blk", "grp"),
        P(),
        P(),
        P(),
        P(),
        P(None, "grp", None),
    )
    return jax.shard_map(
        local,
        mesh=mesh,
        in_specs=placed,
        out_specs=P("blk", "grp", None, None, None),
        check_vma=False,
    )
```

```python
import jax
import jax.numpy as jnp
from jax import lax
from jax.experimental import pallas as pl
from jax.experimental.pallas import tpu as pltpu
from jax.sharding import PartitionSpec as P


BF = jnp.bfloat16
F32 = jnp.float32
VMEM = pltpu.VMEM
SMEM = pltpu.SMEM


def small_vmem(mib):
    return pltpu.CompilerParams(vmem_limit_bytes=mib * 1024 * 1024)


def occupancy(lo, hi, x, y):
    lane = lax.broadcasted_iota(jnp.int32, (8, 128), 1)
    return jnp.where((lane >= lo[x, y]) & (lane < hi[x, y]), 1.0, 0.0)


def masked_column(column, lo, hi, x, y):
    mask = jnp.concatenate([occupancy(lo, hi, x, y)] * 2, axis=0).astype(BF)
    return (column.reshape(4, 16, 128) * mask[None]).reshape(64, 128)


def prep_kernel(
    side, lo, hi, vox, cw, cb, dw, db, x_one, x_two, w_out, d_out, cb_out, db_out, sel_out, sems
):
    core = side[0] & 1
    x_at = (jnp.where(core == 1, 0, 7), jnp.where(core == 1, 7, 0))
    copies = [
        pltpu.make_async_copy(vox.at[x_at[k]], ref, sems.at[k])
        for k, ref in enumerate((x_one, x_two))
    ]
    for copy in copies:
        copy.start()
    zero = jnp.zeros((64, 64), F32)
    for dx in range(3):
        for dz in range(3):
            taps = [cw[dx, dy, dz].astype(F32) for dy in range(3)]
            for yo in range(2):
                line = ([zero] if yo else []) + taps + ([] if yo else [zero])
                for half in range(2):
                    pair = jnp.concatenate(line[2 * half : 2 * half + 2], axis=0)
                    row = (dz * 2 + yo) * 64
                    col = (dx * 4 + half * 2) * 64
                    w_out[row : row + 64, col : col + 128] = pair.T.astype(BF)
    for k in range(2):
        for i in range(2):
            pair = jnp.concatenate([dw[4 * i + k], dw[4 * i + 2 + k]], axis=0).astype(F32)
            d_out[k * 128 : k * 128 + 128, i * 128 : i * 128 + 128] = pair.T.astype(BF)
    cb_out[...] = jnp.broadcast_to(cb[...], (128, 128)).T
    db_out[...] = jnp.broadcast_to(db[...], (128, 128)).T
    for q in range(8):
        z = lax.broadcasted_iota(jnp.int32, (128, 512), 0)
        lane = lax.broadcasted_iota(jnp.int32, (128, 512), 1)
        want = jnp.where(((lane >> 3) & 7) == q, 16 * (lane >> 6) + 2 * (lane & 7), -1)
        sel_out[q * 128 : q * 128 + 128, :] = jnp.where(z == want, 1.0, 0.0).astype(BF)
    for copy, ref, x in zip(copies, (x_one, x_two), x_at):
        copy.wait()
        for y in range(16):
            ref[y] = masked_column(ref[y], lo, hi, x, y)


def prep(side, lo, hi, vox, conv_weight, conv_bias, down_weight, down_bias):
    smem = pl.BlockSpec(memory_space=SMEM)
    vmem = pl.BlockSpec(memory_space=VMEM)
    x_face = jax.ShapeDtypeStruct((16, 64, 128), BF)
    return pl.pallas_call(
        prep_kernel,
        out_shape=(
            x_face,
            x_face,
            jax.ShapeDtypeStruct((384, 768), BF),
            jax.ShapeDtypeStruct((256, 256), BF),
            jax.ShapeDtypeStruct((128, 128), F32),
            jax.ShapeDtypeStruct((128, 128), F32),
            jax.ShapeDtypeStruct((1024, 512), BF),
        ),
        in_specs=[smem] * 3 + [pl.BlockSpec(memory_space=pltpu.HBM)] + [vmem] * 4,
        out_specs=(vmem,) * 7,
        scratch_shapes=[pltpu.SemaphoreType.DMA((2,))],
        compiler_params=small_vmem(8),
        cost_estimate=pl.CostEstimate(flops=10**9, bytes_accessed=4 * 10**6, transcendentals=0),
        name="prep",
    )(
        side,
        *in_place(lo, hi, vox),
        conv_weight,
        jnp.tile(conv_bias, 2)[None],
        down_weight,
        down_bias[None],
    )


def faces_kernel(lo_all, hi_all, vox, y_first, y_last, lo, hi, sems):
    bounds = [
        pltpu.make_async_copy(lo_all, lo, sems.at[0]),
        pltpu.make_async_copy(hi_all, hi, sems.at[1]),
    ]
    copies = [
        pltpu.make_async_copy(vox.at[:, 0], y_first, sems.at[2]),
        pltpu.make_async_copy(vox.at[:, 15], y_last, sems.at[3]),
    ]
    for copy in bounds + copies:
        copy.start()
    for copy in bounds:
        copy.wait()
    for copy, ref, y in zip(copies, (y_first, y_last), (0, 15)):
        copy.wait()
        for x in range(8):
            ref[x] = masked_column(ref[x], lo, hi, x, y)


def in_place(*arrays):
    return tuple(pltpu.with_memory_space_constraint(a, pltpu.HBM) for a in arrays)


def faces(lo, hi, vox):
    y_face = jax.ShapeDtypeStruct((8, 64, 128), BF)
    vmem = pl.BlockSpec(memory_space=VMEM)
    return pl.pallas_call(
        faces_kernel,
        out_shape=(y_face, y_face),
        in_specs=[pl.BlockSpec(memory_space=pltpu.HBM)] * 3,
        out_specs=(vmem, vmem),
        scratch_shapes=[
            SMEM((8, 16), jnp.int32),
            SMEM((8, 16), jnp.int32),
            pltpu.SemaphoreType.DMA((4,)),
        ],
        compiler_params=small_vmem(4),
        name="faces",
    )(*in_place(lo, hi, vox))


def scene_rows(starts, lo, hi, pad, w, d, cb, db, sel, cells):
    lane8 = lax.broadcasted_iota(jnp.int32, (8, 128), 1)
    lane = lax.broadcasted_iota(jnp.int32, (128, 128), 1)

    def conv_cell(row, x, yp):
        rows = [pad[row + r, pl.ds(2 * yp, 4)].reshape(256, 128) for r in range(4)]
        window = jnp.concatenate(
            [jnp.concatenate([rows[t], rows[t + 1]], axis=1) for t in range(3)], axis=0
        )
        summed = jnp.dot(w[...], window, preferred_element_type=F32)
        parts = []
        for xi in range(2):
            part = summed[:, xi * 128 : xi * 128 + 128]
            below = jnp.where(lane == 0, 0.0, pltpu.roll(part[0:128], 1, 1))
            above = jnp.where(lane == 127, 0.0, pltpu.roll(part[256:384], 127, 1))
            half = (below + above + part[128:256] + cb[...]) * 0.5
            act = half + half * jnp.tanh(half)
            masks = [occupancy(lo, hi, x + xi, 2 * yp + yo) for yo in range(2)]
            act = act.reshape(2, 8, 8, 128) * jnp.stack(masks)[:, None]
            parts.append(act.reshape(128, 128).astype(BF))
        return jnp.concatenate(parts, axis=0)

    def coarse_mask(x0, yp):
        found = None
        for xi in range(2):
            for yo in range(2):
                x, y = x0 + xi, 2 * yp + yo
                here = (lane8 + 1 >= lo[x, y]) & (lane8 < hi[x, y])
                found = here if found is None else found | here
        return jnp.where(found, 1.0, 0.0)

    (row0, x0), (row1, x1) = starts

    for t in range(2):
        row = row0 + t * (row1 - row0)
        x = x0 + t * (x1 - x0)
        for ypp in range(4):
            hidden = jnp.concatenate(
                [conv_cell(row, x, 2 * ypp), conv_cell(row, x, 2 * ypp + 1)], axis=1
            )
            down = jnp.dot(d[...], hidden, preferred_element_type=F32)
            for e in range(2):
                q = 2 * ypp + e
                part = down[:, e * 128 : e * 128 + 128]
                total = part[0:128] + pltpu.roll(part[128:256], 127, 1) + db[...]
                total = total.reshape(16, 8, 128) * coarse_mask(x, q)[None]
                cells[t * 128 : t * 128 + 128, q * 128 : q * 128 + 128] = total.reshape(
                    128, 128
                ).astype(BF)

    return jnp.dot(cells[...], sel[...], preferred_element_type=F32)


def inner_kernel(side, lo, hi, vox, y_one, y_two, w, d, cb, db, sel, out, pad, cells):
    odd = side[0] >> 1
    one_at, two_at = 17 * (1 - odd), 17 * odd
    for r in range(6):
        pad[r, one_at] = y_one[r + 1]
        pad[r, two_at] = y_two[r + 1]

    @pl.loop(0, 6)
    def _(r):
        for y in range(16):
            pad[r, y + 1] = masked_column(vox[r + 1, y], lo, hi, r + 1, y)

    out[...] = scene_rows(((0, 2), (2, 4)), lo, hi, pad, w, d, cb, db, sel, cells)


def outer_kernel(
    side, lo, hi, slots, vox, y_one, y_two, x_one, x_two, inner, w, d, cb, db, sel, keep, give, pad, cells, pieces
):
    core, odd = side[0] & 1, side[0] >> 1
    one_at, two_at = 17 * (1 - odd), 17 * odd
    pad[7 * (1 - core)] = x_one[...]
    pad[7 * core] = x_two[...]
    for r in range(3):
        pad[r + 1, one_at] = y_one[r]
        pad[r + 1, two_at] = y_two[r]
        pad[r + 4, one_at] = y_one[r + 5]
        pad[r + 4, two_at] = y_two[r + 5]

    @pl.loop(0, 3)
    def _(r):
        for y in range(16):
            pad[r + 1, y + 1] = masked_column(vox[r, y], lo, hi, r, y)
            pad[r + 4, y + 1] = masked_column(vox[r + 5, y], lo, hi, r + 5, y)

    ends = scene_rows(((0, 0), (4, 6)), lo, hi, pad, w, d, cb, db, sel, cells)
    rows = (ends[0:128], inner[0:128], inner[128:256], ends[128:256])
    for pair in range(2):
        for level in range(8):
            at = slice(level * 64, level * 64 + 64)
            both = jnp.concatenate([rows[2 * pair][:, at], rows[2 * pair + 1][:, at]], axis=1)
            pieces[slots[level], :, pair * 128 : pair * 128 + 128] = both.astype(BF)
    keep[...] = pieces[0:4]
    give[...] = pieces[4:8]


def inner_rows(side, lo, hi, vox, y_one, y_two, tables):
    smem = pl.BlockSpec(memory_space=SMEM)
    vmem = pl.BlockSpec(memory_space=VMEM)
    return pl.pallas_call(
        inner_kernel,
        out_shape=jax.ShapeDtypeStruct((256, 512), F32),
        in_specs=[smem] * 3 + [vmem] * 8,
        out_specs=vmem,
        scratch_shapes=[VMEM((6, 18, 64, 128), BF), VMEM((256, 1024), BF)],
        compiler_params=small_vmem(12),
        cost_estimate=pl.CostEstimate(flops=5 * 10**9, bytes_accessed=4 * 10**6, transcendentals=0),
        name="inner",
    )(side, lo, hi, vox, y_one, y_two, *tables)


def outer_rows(side, lo, hi, slots, vox, y_one, y_two, x_one, x_two, inner, tables):
    half = jax.ShapeDtypeStruct((4, 128, 256), BF)
    smem = pl.BlockSpec(memory_space=SMEM)
    vmem = pl.BlockSpec(memory_space=VMEM)
    return pl.pallas_call(
        outer_kernel,
        out_shape=(half, half),
        in_specs=[smem] * 4 + [vmem] * 11,
        out_specs=(vmem, vmem),
        scratch_shapes=[
            VMEM((8, 18, 64, 128), BF),
            VMEM((256, 1024), BF),
            VMEM((8, 128, 256), BF),
        ],
        compiler_params=small_vmem(12),
        name="outer",
    )(side, lo, hi, slots, vox, y_one, y_two, x_one, x_two, inner, *tables)


def ring(count, step):
    return [(i, step(i) % count) for i in range(count)]


def local(voxels, shell_lo, shell_hi, conv_weight, conv_bias, down_weight, down_bias, coarse_owner):
    blk_n = lax.axis_size("blk")
    grp_n = lax.axis_size("grp")
    me = lax.axis_index("blk")
    core = me % 2

    grp_odd = lax.axis_index("grp") % 2
    side = (core + 2 * grp_odd).astype(jnp.int32).reshape(1)

    def swaps(count, first):
        lower = range(first, count - 1, 2)
        return [(i, i + 1) for i in lower] + [(i + 1, i) for i in lower]

    y_first, y_last = faces(shell_lo, shell_hi, voxels)
    y_one = jnp.where(grp_odd == 1, y_first, y_last)
    y_two = jnp.where(grp_odd == 1, y_last, y_first)
    y_one = lax.ppermute(y_one, "grp", swaps(grp_n, 0))
    y_two = lax.ppermute(y_two, "grp", swaps(grp_n, 1))
    x_one, x_two, *tables = prep(
        side, shell_lo, shell_hi, voxels, conv_weight, conv_bias, down_weight, down_bias
    )
    y_one, y_two, tables = lax.optimization_barrier((y_one, y_two, tuple(tables)))

    def x_message(face, last_row):
        ones = jnp.where(last_row, y_one[7:8], y_one[0:1])
        twos = jnp.where(last_row, y_two[7:8], y_two[0:1])
        low = jnp.where(grp_odd == 1, ones, twos)
        high = jnp.where(grp_odd == 1, twos, ones)
        return jnp.concatenate([low, face, high])

    x_one = lax.ppermute(x_message(x_one, core == 0), "blk", swaps(blk_n, 0))
    x_two = lax.ppermute(x_message(x_two, core == 1), "blk", swaps(blk_n, 1))
    inner = inner_rows(side, shell_lo, shell_hi, voxels, y_one, y_two, tables)

    column = me // 2
    owners = lax.dynamic_index_in_dim(coarse_owner[:, 0, :], column, 0, keepdims=False)
    offset = (owners - 2 * column + 3) % blk_n
    slots = (offset + 4 * core) % 8

    keep, give = outer_rows(
        side, shell_lo, shell_hi, slots, voxels, y_one, y_two, x_one, x_two, inner, tables
    )
    got = lax.ppermute(give, "blk", ring(blk_n, lambda i: i ^ 1))
    even = core == 0
    whole = jnp.where(
        even, jnp.concatenate([keep, got], axis=2), jnp.concatenate([got, keep], axis=2)
    )

    def mine(a, b):
        return jnp.where(even, whole[a], whole[b])

    pairs = ring(blk_n, lambda i: i + 1 if i % 2 else i - 1)
    one = lax.ppermute(mine(2, 1), "blk", pairs)
    pairs = ring(blk_n, lambda i: i + 3 if i % 2 else i - 3)
    three = lax.ppermute(mine(0, 3), "blk", pairs)
    pairs = ring(blk_n, lambda i: i + 2 if i % 2 else i - 2)
    two = lax.ppermute(mine(1, 2), "blk", pairs)
    stay = mine(3, 0)
    result = jnp.where(
        even, jnp.stack([three, one, stay, two]), jnp.stack([two, stay, one, three])
    )
    return result[None, None]


def solution(mesh):
    placed = (
        P("blk", "grp", None, None),
        P("blk", "grp"),
        P("blk", "grp"),
        P(),
        P(),
        P(),
        P(),
        P(None, "grp", None),
    )
    return jax.shard_map(
        local,
        mesh=mesh,
        in_specs=placed,
        out_specs=P("blk", "grp", None, None, None),
        check_vma=False,
    )
```

```python
import jax
import jax.numpy as jnp
from jax import lax
from jax.experimental import pallas as pl
from jax.experimental.pallas import tpu as pltpu
from jax.sharding import PartitionSpec as P


BF = jnp.bfloat16
F32 = jnp.float32
VMEM = pltpu.VMEM
SMEM = pltpu.SMEM


def small_vmem(mib):
    return pltpu.CompilerParams(vmem_limit_bytes=mib * 1024 * 1024)


def occupancy(lo, hi, x, y):
    lane = lax.broadcasted_iota(jnp.int32, (8, 128), 1)
    return jnp.where((lane >= lo[x, y]) & (lane < hi[x, y]), 1.0, 0.0)


def masked_column(column, lo, hi, x, y):
    mask = jnp.concatenate([occupancy(lo, hi, x, y)] * 2, axis=0).astype(BF)
    return (column.reshape(4, 16, 128) * mask[None]).reshape(64, 128)


def prep_kernel(
    side, lo, hi, vox, cw, cb, dw, db, x_one, x_two, w_out, d_out, cb_out, db_out, sel_out, sems
):
    core = side[0] & 1
    x_at = (jnp.where(core == 1, 0, 7), jnp.where(core == 1, 7, 0))
    copies = [
        pltpu.make_async_copy(vox.at[x_at[k]], ref, sems.at[k])
        for k, ref in enumerate((x_one, x_two))
    ]
    for copy in copies:
        copy.start()
    zero = jnp.zeros((64, 64), F32)
    for dx in range(3):
        for dz in range(3):
            taps = [cw[dx, dy, dz].astype(F32) for dy in range(3)]
            for yo in range(2):
                line = ([zero] if yo else []) + taps + ([] if yo else [zero])
                for half in range(2):
                    pair = jnp.concatenate(line[2 * half : 2 * half + 2], axis=0)
                    row = (dz * 2 + yo) * 64
                    col = (dx * 4 + half * 2) * 64
                    w_out[row : row + 64, col : col + 128] = pair.T.astype(BF)
    for k in range(2):
        for i in range(2):
            pair = jnp.concatenate([dw[4 * i + k], dw[4 * i + 2 + k]], axis=0).astype(F32)
            d_out[k * 128 : k * 128 + 128, i * 128 : i * 128 + 128] = pair.T.astype(BF)
    cb_out[...] = jnp.broadcast_to(cb[...], (128, 128)).T
    db_out[...] = jnp.broadcast_to(db[...], (128, 128)).T
    for q in range(8):
        z = lax.broadcasted_iota(jnp.int32, (128, 512), 0)
        lane = lax.broadcasted_iota(jnp.int32, (128, 512), 1)
        want = jnp.where(((lane >> 3) & 7) == q, 16 * (lane >> 6) + 2 * (lane & 7), -1)
        sel_out[q * 128 : q * 128 + 128, :] = jnp.where(z == want, 1.0, 0.0).astype(BF)
    for copy, ref, x in zip(copies, (x_one, x_two), x_at):
        copy.wait()
        for y in range(16):
            ref[y] = masked_column(ref[y], lo, hi, x, y)


def prep(side, lo, hi, vox, conv_weight, conv_bias, down_weight, down_bias):
    smem = pl.BlockSpec(memory_space=SMEM)
    vmem = pl.BlockSpec(memory_space=VMEM)
    x_face = jax.ShapeDtypeStruct((16, 64, 128), BF)
    return pl.pallas_call(
        prep_kernel,
        out_shape=(
            x_face,
            x_face,
            jax.ShapeDtypeStruct((384, 768), BF),
            jax.ShapeDtypeStruct((256, 256), BF),
            jax.ShapeDtypeStruct((128, 128), F32),
            jax.ShapeDtypeStruct((128, 128), F32),
            jax.ShapeDtypeStruct((1024, 512), BF),
        ),
        in_specs=[smem] * 3 + [pl.BlockSpec(memory_space=pltpu.HBM)] + [vmem] * 4,
        out_specs=(vmem,) * 7,
        scratch_shapes=[pltpu.SemaphoreType.DMA((2,))],
        compiler_params=small_vmem(8),
        cost_estimate=pl.CostEstimate(flops=10**9, bytes_accessed=4 * 10**6, transcendentals=0),
        name="prep",
    )(
        side,
        *in_place(lo, hi, vox),
        conv_weight,
        jnp.tile(conv_bias, 2)[None],
        down_weight,
        down_bias[None],
    )


def faces_kernel(lo_all, hi_all, vox, y_first, y_last, lo, hi, sems):
    bounds = [
        pltpu.make_async_copy(lo_all, lo, sems.at[0]),
        pltpu.make_async_copy(hi_all, hi, sems.at[1]),
    ]
    copies = [
        pltpu.make_async_copy(vox.at[:, 0], y_first, sems.at[2]),
        pltpu.make_async_copy(vox.at[:, 15], y_last, sems.at[3]),
    ]
    for copy in bounds + copies:
        copy.start()
    for copy in bounds:
        copy.wait()
    for copy, ref, y in zip(copies, (y_first, y_last), (0, 15)):
        copy.wait()
        for x in range(8):
            ref[x] = masked_column(ref[x], lo, hi, x, y)


def in_place(*arrays):
    return tuple(pltpu.with_memory_space_constraint(a, pltpu.HBM) for a in arrays)


def faces(lo, hi, vox):
    y_face = jax.ShapeDtypeStruct((8, 64, 128), BF)
    vmem = pl.BlockSpec(memory_space=VMEM)
    return pl.pallas_call(
        faces_kernel,
        out_shape=(y_face, y_face),
        in_specs=[pl.BlockSpec(memory_space=pltpu.HBM)] * 3,
        out_specs=(vmem, vmem),
        scratch_shapes=[
            SMEM((8, 16), jnp.int32),
            SMEM((8, 16), jnp.int32),
            pltpu.SemaphoreType.DMA((4,)),
        ],
        compiler_params=small_vmem(4),
        name="faces",
    )(*in_place(lo, hi, vox))


def scene_rows(starts, lo, hi, pad, w, d, cb, db, sel, cells):
    lane8 = lax.broadcasted_iota(jnp.int32, (8, 128), 1)
    lane = lax.broadcasted_iota(jnp.int32, (128, 128), 1)

    def conv_cell(row, x, yp):
        rows = [pad[row + r, pl.ds(2 * yp, 4)].reshape(256, 128) for r in range(4)]
        window = jnp.concatenate(
            [jnp.concatenate([rows[t], rows[t + 1]], axis=1) for t in range(3)], axis=0
        )
        summed = jnp.dot(w[...], window, preferred_element_type=F32)
        parts = []
        for xi in range(2):
            part = summed[:, xi * 128 : xi * 128 + 128]
            below = jnp.where(lane == 0, 0.0, pltpu.roll(part[0:128], 1, 1))
            above = jnp.where(lane == 127, 0.0, pltpu.roll(part[256:384], 127, 1))
            half = (below + above + part[128:256] + cb[...]) * 0.5
            act = half + half * jnp.tanh(half)
            masks = [occupancy(lo, hi, x + xi, 2 * yp + yo) for yo in range(2)]
            act = act.reshape(2, 8, 8, 128) * jnp.stack(masks)[:, None]
            parts.append(act.reshape(128, 128).astype(BF))
        return jnp.concatenate(parts, axis=0)

    def coarse_mask(x0, yp):
        found = None
        for xi in range(2):
            for yo in range(2):
                x, y = x0 + xi, 2 * yp + yo
                here = (lane8 + 1 >= lo[x, y]) & (lane8 < hi[x, y])
                found = here if found is None else found | here
        return jnp.where(found, 1.0, 0.0)

    (row0, x0), (row1, x1) = starts

    for t in range(2):
        row = row0 + t * (row1 - row0)
        x = x0 + t * (x1 - x0)
        for ypp in range(4):
            hidden = jnp.concatenate(
                [conv_cell(row, x, 2 * ypp), conv_cell(row, x, 2 * ypp + 1)], axis=1
            )
            down = jnp.dot(d[...], hidden, preferred_element_type=F32)
            for e in range(2):
                q = 2 * ypp + e
                part = down[:, e * 128 : e * 128 + 128]
                total = part[0:128] + pltpu.roll(part[128:256], 127, 1) + db[...]
                total = total.reshape(16, 8, 128) * coarse_mask(x, q)[None]
                cells[t * 128 : t * 128 + 128, q * 128 : q * 128 + 128] = total.reshape(
                    128, 128
                ).astype(BF)

    return jnp.dot(cells[...], sel[...], preferred_element_type=F32)


def fetch_bounds(lo_all, hi_all, lo, hi, sems):
    copies = [
        pltpu.make_async_copy(lo_all, lo, sems.at[0]),
        pltpu.make_async_copy(hi_all, hi, sems.at[1]),
    ]
    for copy in copies:
        copy.start()
    return copies


BOUNDS = [
    SMEM((8, 16), jnp.int32),
    SMEM((8, 16), jnp.int32),
    pltpu.SemaphoreType.DMA((2,)),
]


def inner_kernel(
    side, lo_all, hi_all, vox, y_one, y_two, w, d, cb, db, sel, out, pad, cells, lo, hi, sems
):
    bounds = fetch_bounds(lo_all, hi_all, lo, hi, sems)
    odd = side[0] >> 1
    one_at, two_at = 17 * (1 - odd), 17 * odd
    for r in range(6):
        pad[r, one_at] = y_one[r + 1]
        pad[r, two_at] = y_two[r + 1]
    for copy in bounds:
        copy.wait()

    @pl.loop(0, 6)
    def _(r):
        for y in range(16):
            pad[r, y + 1] = masked_column(vox[r + 1, y], lo, hi, r + 1, y)

    out[...] = scene_rows(((0, 2), (2, 4)), lo, hi, pad, w, d, cb, db, sel, cells)


def outer_kernel(
    side, lo_all, hi_all, slots, vox, y_one, y_two, x_one, x_two, inner, w, d, cb, db, sel,
    keep, give, pad, cells, pieces, lo, hi, sems
):
    bounds = fetch_bounds(lo_all, hi_all, lo, hi, sems)
    core, odd = side[0] & 1, side[0] >> 1
    one_at, two_at = 17 * (1 - odd), 17 * odd
    pad[7 * (1 - core)] = x_one[...]
    pad[7 * core] = x_two[...]
    for r in range(3):
        pad[r + 1, one_at] = y_one[r]
        pad[r + 1, two_at] = y_two[r]
        pad[r + 4, one_at] = y_one[r + 5]
        pad[r + 4, two_at] = y_two[r + 5]
    for copy in bounds:
        copy.wait()

    @pl.loop(0, 3)
    def _(r):
        for y in range(16):
            pad[r + 1, y + 1] = masked_column(vox[r, y], lo, hi, r, y)
            pad[r + 4, y + 1] = masked_column(vox[r + 5, y], lo, hi, r + 5, y)

    ends = scene_rows(((0, 0), (4, 6)), lo, hi, pad, w, d, cb, db, sel, cells)
    rows = (ends[0:128], inner[0:128], inner[128:256], ends[128:256])
    for pair in range(2):
        for level in range(8):
            at = slice(level * 64, level * 64 + 64)
            both = jnp.concatenate([rows[2 * pair][:, at], rows[2 * pair + 1][:, at]], axis=1)
            pieces[slots[level], :, pair * 128 : pair * 128 + 128] = both.astype(BF)
    keep[...] = pieces[0:4]
    give[...] = pieces[4:8]


def inner_rows(side, lo, hi, vox, y_one, y_two, tables):
    smem = pl.BlockSpec(memory_space=SMEM)
    vmem = pl.BlockSpec(memory_space=VMEM)
    return pl.pallas_call(
        inner_kernel,
        out_shape=jax.ShapeDtypeStruct((256, 512), F32),
        in_specs=[smem] + [pl.BlockSpec(memory_space=pl.ANY)] * 2 + [vmem] * 8,
        out_specs=vmem,
        scratch_shapes=[VMEM((6, 18, 64, 128), BF), VMEM((256, 1024), BF), *BOUNDS],
        compiler_params=small_vmem(12),
        cost_estimate=pl.CostEstimate(flops=5 * 10**9, bytes_accessed=4 * 10**6, transcendentals=0),
        name="inner",
    )(side, lo, hi, vox, y_one, y_two, *tables)


def outer_rows(side, lo, hi, slots, vox, y_one, y_two, x_one, x_two, inner, tables):
    half = jax.ShapeDtypeStruct((4, 128, 256), BF)
    smem = pl.BlockSpec(memory_space=SMEM)
    vmem = pl.BlockSpec(memory_space=VMEM)
    return pl.pallas_call(
        outer_kernel,
        out_shape=(half, half),
        in_specs=[smem] + [pl.BlockSpec(memory_space=pl.ANY)] * 2 + [smem] + [vmem] * 11,
        out_specs=(vmem, vmem),
        scratch_shapes=[
            VMEM((8, 18, 64, 128), BF),
            VMEM((256, 1024), BF),
            VMEM((8, 128, 256), BF),
            *BOUNDS,
        ],
        compiler_params=small_vmem(12),
        name="outer",
    )(side, lo, hi, slots, vox, y_one, y_two, x_one, x_two, inner, *tables)


def ring(count, step):
    return [(i, step(i) % count) for i in range(count)]


def local(voxels, shell_lo, shell_hi, conv_weight, conv_bias, down_weight, down_bias, coarse_owner):
    blk_n = lax.axis_size("blk")
    grp_n = lax.axis_size("grp")
    me = lax.axis_index("blk")
    core = me % 2

    grp_odd = lax.axis_index("grp") % 2
    side = (core + 2 * grp_odd).astype(jnp.int32).reshape(1)

    def swaps(count, first):
        lower = range(first, count - 1, 2)
        return [(i, i + 1) for i in lower] + [(i + 1, i) for i in lower]

    y_first, y_last = faces(shell_lo, shell_hi, voxels)
    y_one = jnp.where(grp_odd == 1, y_first, y_last)
    y_two = jnp.where(grp_odd == 1, y_last, y_first)
    y_one = lax.ppermute(y_one, "grp", swaps(grp_n, 0))
    y_two = lax.ppermute(y_two, "grp", swaps(grp_n, 1))
    x_one, x_two, *tables = prep(
        side, shell_lo, shell_hi, voxels, conv_weight, conv_bias, down_weight, down_bias
    )
    y_one, y_two, tables = lax.optimization_barrier((y_one, y_two, tuple(tables)))

    def x_message(face, last_row):
        ones = jnp.where(last_row, y_one[7:8], y_one[0:1])
        twos = jnp.where(last_row, y_two[7:8], y_two[0:1])
        low = jnp.where(grp_odd == 1, ones, twos)
        high = jnp.where(grp_odd == 1, twos, ones)
        return jnp.concatenate([low, face, high])

    x_one = lax.ppermute(x_message(x_one, core == 0), "blk", swaps(blk_n, 0))
    x_two = lax.ppermute(x_message(x_two, core == 1), "blk", swaps(blk_n, 1))
    inner = inner_rows(side, shell_lo, shell_hi, voxels, y_one, y_two, tables)

    column = me // 2
    owners = lax.dynamic_index_in_dim(coarse_owner[:, 0, :], column, 0, keepdims=False)
    offset = (owners - 2 * column + 3) % blk_n
    slots = (offset + 4 * core) % 8

    keep, give = outer_rows(
        side, shell_lo, shell_hi, slots, voxels, y_one, y_two, x_one, x_two, inner, tables
    )
    got = lax.ppermute(give, "blk", ring(blk_n, lambda i: i ^ 1))
    even = core == 0
    whole = jnp.where(
        even, jnp.concatenate([keep, got], axis=2), jnp.concatenate([got, keep], axis=2)
    )

    def mine(a, b):
        return jnp.where(even, whole[a], whole[b])

    pairs = ring(blk_n, lambda i: i + 1 if i % 2 else i - 1)
    one = lax.ppermute(mine(2, 1), "blk", pairs)
    pairs = ring(blk_n, lambda i: i + 3 if i % 2 else i - 3)
    three = lax.ppermute(mine(0, 3), "blk", pairs)
    pairs = ring(blk_n, lambda i: i + 2 if i % 2 else i - 2)
    two = lax.ppermute(mine(1, 2), "blk", pairs)
    stay = mine(3, 0)
    result = jnp.where(
        even, jnp.stack([three, one, stay, two]), jnp.stack([two, stay, one, three])
    )
    return result[None, None]


def solution(mesh):
    placed = (
        P("blk", "grp", None, None),
        P("blk", "grp"),
        P("blk", "grp"),
        P(),
        P(),
        P(),
        P(),
        P(None, "grp", None),
    )
    return jax.shard_map(
        local,
        mesh=mesh,
        in_specs=placed,
        out_specs=P("blk", "grp", None, None, None),
        check_vma=False,
    )
```
